128 devices in a mesh: dir: 2 (over x_lo), shard: 64 (over x_hi, y, z, core).
Axes of the slice: x: 4 (x_hi: 2, x_lo: 2; x = x_hi * 2 + x_lo), y: 4, z: 4, core: 2. Of those that a mesh axis runs over, the one named last changes fastest.
Arguments:
- propagators: bfloat16 [2, 512, 64, 1024], P('dir', 'shard'), may hold values from 0.5 to 1.5
- field: float32 [64, 1024], replicated, may hold values from -0.5 to 0.5
- orient: float32 [3, 512], replicated, may hold values from -1 to 1, as said below
- quad_weights: float32 [512], replicated, may hold values from 0.01 to 0.1
- analysis: bfloat16 [441, 512], replicated, may hold values from -0.25 to 0.25
- synthesis: bfloat16 [512, 441], replicated, may hold values from -0.4375 to 0.4375
- decay: float32 [441], replicated, may hold values from 0.5 to 1
Outputs:
- density: float32 [64, 1024], P('shard', 'dir')
- qtensor: float32 [5, 64, 1024], P(None, 'shard', 'dir')
The draws below stay inside these ranges and needn't reach their ends.
Inputs may be any that keep to these rules, and one draw needn't show every extreme that they name: Each column of orient is a unit vector.
All inputs are finite; a program needn't handle non-finite values.
Results may differ from the reference program's by a relative error of at most 0.028.
Values may be sent and summed in bfloat16 or wider, within the bound.
No kernel may reach another device: no remote copies, remote signals or barrier semaphores. Data moves between devices by JAX's collectives and lax.ppermute only.
A program may use at most 128 MiB of HBM per device.

```python
import math
import jax
import jax.numpy as jnp
from jax import lax

NX = 64
NY = 64
NZ = 16
M = 512
H = 441
STEPS = 2


def draw_orient(key, part):
    polar_key = jax.random.fold_in(key, 11)
    azimuth_key = jax.random.fold_in(key, 12)
    cosine = jax.random.uniform(polar_key, (M,), jnp.float32, -1.0, 1.0)
    azimuth = jax.random.uniform(azimuth_key, (M,), jnp.float32, -math.pi, math.pi)
    sine_polar = jnp.sqrt(jnp.maximum(1.0 - cosine * cosine, 0.0))
    return jnp.stack([sine_polar * jnp.cos(azimuth), sine_polar * jnp.sin(azimuth), cosine])


def block_levels(own_key, extent, split, least, high):
    loudness = 1.0
    for axis_at, blocks in split:
        draws = jax.random.uniform(jax.random.fold_in(jax.random.fold_in(own_key, 6), axis_at), (blocks,), jnp.float32, least / len(split), high / len(split))
        loudness = loudness * jnp.repeat(jnp.exp(draws), extent[axis_at] // blocks).reshape((-1,) + (1,) * (len(extent) - 1 - axis_at))
    return loudness


def gaussian(rng, extent, scale, most, held_as=jnp.bfloat16):
    entries = jax.random.normal(rng, extent, jnp.float32) * scale
    return jnp.minimum(jnp.maximum(entries, -most), most).astype(held_as)


def setup_inputs(seed: int = 0) -> dict:
    key_list = jax.random.split(jax.random.key(seed), 8)
    propagators = jnp.clip(0.5 + 1.0 * jax.random.uniform(key_list[0], (2, M, NX, NY * NZ), jnp.float32) ** block_levels(key_list[0], (2, M, NX, NY * NZ), ((0, 2), (1, 64)), -0.2, 0.2), 0.5, 1.5).astype(jnp.bfloat16)
    field = jnp.clip(jax.random.uniform(key_list[1], (NX, NY * NZ), jnp.float32, -0.5, 0.5), -0.5, 0.5)
    orient = draw_orient(jax.random.fold_in(key_list[7], 71), 0)
    quad_weights = jnp.clip(jnp.exp(jax.random.uniform(key_list[3], (M,), jnp.float32, math.log(0.01), math.log(0.1))), 0.01, 0.1)
    analysis = gaussian(key_list[4], (H, M), M ** -0.5, 0.25)
    synthesis = gaussian(key_list[5], (M, H), (H // 2) ** -0.5, 0.4375)
    decay = jnp.clip(jnp.exp(jax.random.uniform(key_list[6], (H,), jnp.float32, math.log(0.5), math.log(1.0))), 0.5, 1.0)
    return {"propagators": propagators, "field": field, "orient": orient, "quad_weights": quad_weights, "analysis": analysis, "synthesis": synthesis, "decay": decay}


transport_length = 1.5
one_third = 1.0 / 3.0
patterns = {1: "kx,mxyz->mkyz", 2: "ky,mxyz->mxkz", 3: "kz,mxyz->mxyk"}


def dft_tables(length):
    counter = jnp.arange(length, dtype=jnp.int32)
    wrapped = (counter[:, None] * counter[None, :]) % length
    angles = wrapped.astype(jnp.float32) * (2.0 * math.pi / length)
    return jnp.cos(angles).astype(jnp.bfloat16), jnp.sin(angles).astype(jnp.bfloat16)


def wave_numbers(length):
    counter = jnp.arange(length, dtype=jnp.int32)
    signed = jnp.where(counter <= (length - 1) // 2, counter, counter - length)
    return signed.astype(jnp.float32) * (2.0 * math.pi / length)


def phases(heading, direction, lengths):
    wave_x = wave_numbers(lengths[0])[None, :, None, None]
    wave_y = wave_numbers(lengths[1])[None, None, :, None]
    wave_z = wave_numbers(lengths[2])[None, None, None, :]
    phase_angle = (heading[0][:, None, None, None] * wave_x + heading[1][:, None, None, None] * wave_y
                   + heading[2][:, None, None, None] * wave_z) * (direction * transport_length)
    return jnp.cos(phase_angle), jnp.sin(phase_angle)


def along_axis(table, values, position):
    return jnp.einsum(patterns[position], table.astype(jnp.float32), values.astype(jnp.float32))


def complex_pass(tables, real_part, imag_part, position, turning):
    cosine_table, sine_table = tables
    new_real = along_axis(cosine_table, real_part, position) - turning * along_axis(sine_table, imag_part, position)
    new_imag = along_axis(cosine_table, imag_part, position) + turning * along_axis(sine_table, real_part, position)
    return new_real.astype(jnp.bfloat16), new_imag.astype(jnp.bfloat16)


def transport(values, dft_sets, cos_phase, sin_phase, damping):
    cos_x, sin_x = dft_sets[0]
    real_part = along_axis(cos_x, values, 1).astype(jnp.bfloat16)
    imag_part = (-along_axis(sin_x, values, 1)).astype(jnp.bfloat16)
    real_part, imag_part = complex_pass(dft_sets[1], real_part, imag_part, 2, -1.0)
    real_part, imag_part = complex_pass(dft_sets[2], real_part, imag_part, 3, -1.0)
    real_wide = real_part.astype(jnp.float32)
    imag_wide = imag_part.astype(jnp.float32)
    real_part = (real_wide * cos_phase + imag_wide * sin_phase).astype(jnp.bfloat16)
    imag_part = (imag_wide * cos_phase - real_wide * sin_phase).astype(jnp.bfloat16)
    real_part, imag_part = complex_pass(dft_sets[2], real_part, imag_part, 3, 1.0)
    real_part, imag_part = complex_pass(dft_sets[1], real_part, imag_part, 2, 1.0)
    summed = along_axis(cos_x, real_part, 1) - along_axis(sin_x, imag_part, 1)
    return (summed * damping[None]).astype(jnp.bfloat16)


def diffuse(points, analysis, synthesis, decay):
    layout = points.shape
    columns = points.reshape(layout[0], -1)
    harmonic_part = jnp.dot(analysis, columns, preferred_element_type=jnp.float32)
    harmonic_part = (harmonic_part * decay[:, None]).astype(jnp.bfloat16)
    return jnp.dot(synthesis, harmonic_part, preferred_element_type=jnp.float32).astype(jnp.bfloat16).reshape(layout)


def moment_table(orient, quad_weights):
    head_x, head_y, head_z = orient[0], orient[1], orient[2]
    unity = jnp.ones_like(head_x)
    moment_rows = [unity, head_x * head_x - one_third, head_y * head_y - one_third,
                   head_x * head_y, head_x * head_z, head_y * head_z]
    return jnp.stack(moment_rows) * quad_weights[None, :]


def reference(propagators, field, orient, quad_weights, analysis, synthesis, decay):
    propagators = propagators.reshape(2, M, NX, NY, NZ)
    field = field.reshape(NX, NY, NZ)
    dft_sets = [dft_tables(NX), dft_tables(NY), dft_tables(NZ)]
    damping = jnp.exp(-field) / float(NX * NY * NZ)
    block_width = math.gcd(M, 32)
    blocks = M // block_width
    headings = orient.reshape(3, blocks, block_width).transpose(1, 0, 2)

    def advance(state, direction):
        def advance_block(member):
            values, heading = member
            cos_phase, sin_phase = phases(heading, direction, (NX, NY, NZ))
            return transport(values, dft_sets, cos_phase, sin_phase, damping)

        moved = lax.map(advance_block, (state.reshape(blocks, block_width, NX, NY, NZ), headings))
        moved = moved.reshape(M, NX, NY, NZ)
        planes = jnp.moveaxis(moved, 1, 0).reshape(NX, M, NY * NZ)

        def mix_plane(values):
            return diffuse(values, analysis, synthesis, decay)

        diffused = lax.map(mix_plane, planes)
        return jnp.moveaxis(diffused.reshape(NX, M, NY, NZ), 0, 1)

    forward = propagators[0]
    backward = propagators[1]
    for contour in range(STEPS):
        forward = advance(forward, 1.0)
        backward = advance(backward, -1.0)
    product = forward.astype(jnp.float32).reshape(M, -1) * backward.astype(jnp.float32).reshape(M, -1)
    result = jnp.dot(moment_table(orient, quad_weights), product, precision=lax.Precision.HIGHEST)
    return result[0].reshape(NX, NY * NZ), result[1:].reshape(5, NX, NY * NZ)
```

```python
import functools
import math

import jax
import jax.numpy as jnp
import numpy as np
from jax import lax
from jax.experimental import pallas as pl
from jax.experimental.pallas import tpu as pltpu
from jax.sharding import PartitionSpec as P

NX = 64
NY = 64
NZ = 16
M = 512
CELLS = NY * NZ
SHARDS = 64
LOCAL = M // SHARDS
TRANSPORT = 1.5
THIRD = 1.0 / 3.0
BF = jnp.bfloat16
F32 = jnp.float32
NYQUIST_ROWS = 80
VMEM_LIMIT = 56 * 1024 * 1024


def slot_list():
    plain, nyquist = [], []
    for kz in range(1, 8):
        for ky in range(64):
            (nyquist if ky == 32 else plain).append(((ky, kz), (ky, kz), True))
    for ky in range(1, 32):
        plain.append(((ky, 0), (ky, 0), True))
        nyquist.append(((ky, 8), (ky, 8), True))
    nyquist.append(((0, 0), (0, 8), False))
    nyquist.append(((32, 0), (32, 8), False))
    return plain + nyquist


def point_waves(point):
    ky, kz = point
    fy = ky if ky <= 31 else ky - 64
    fz = kz if kz <= 7 else kz - 16
    rest = (0.0 if ky == 32 else fy / 64.0, 0.0 if kz == 8 else fz / 16.0)
    nyq = (-0.5 if ky == 32 else 0.0, -0.5 if kz == 8 else 0.0)
    return rest, nyq


@functools.lru_cache(maxsize=None)
def tables():
    slots = slot_list()
    y = np.arange(64)[:, None]
    z = np.arange(16)[None, :]
    forward = np.zeros((64, 2, 8, CELLS))
    weight = np.zeros((64, 2, 8))
    waves = np.zeros((8, 512), np.float32)
    for at, (re_point, im_point, paired) in enumerate(slots):
        group, slot = divmod(at, 8)
        for part, point in enumerate((re_point, im_point)):
            angle = 2.0 * math.pi * (((point[0] * y) % 64) / 64.0 + ((point[1] * z) % 16) / 16.0)
            row = -np.sin(angle) if (paired and part == 1) else np.cos(angle)
            forward[group, part, slot] = row.reshape(-1)
            weight[group, part, slot] = (2.0 if paired else 1.0) / CELLS
            rest, nyq = point_waves(point)
            waves[2 * part, at], waves[2 * part + 1, at] = rest
            waves[4 + 2 * part, at], waves[5 + 2 * part, at] = nyq
    forward = forward.reshape(1024, CELLS)
    weight = weight.reshape(1024)
    inverse = forward.T * weight[None, :]
    x = np.arange(64)[:, None]
    j = np.arange(32)[None, :]
    angle = 2.0 * math.pi * ((x * j) % 64) / 64.0
    cosine = np.cos(angle)
    sine = -np.sin(angle)
    partner_c, partner_s = sine.copy(), -cosine
    sine[:, 0] = (-1.0) ** np.arange(64)
    partner_s[:, 0] = 0.0
    partner_c[:, 0] = 0.0
    fx = np.concatenate([cosine, sine], 1)
    fx_partner = np.concatenate([partner_c, partner_s], 1)
    wx = np.full(64, 2.0 / 64)
    wx[0] = wx[32] = 1.0 / 64
    fx_inv = (fx * wx[None, :]).T
    return dict(forward=forward, inverse=inverse, waves=waves, fx=fx, fxp=fx_partner, fxi=fx_inv)


def turns_cos(t):
    return turns_sin(t + 0.25)


def turns_sin(t):
    r = t - jnp.round(t)
    r = jnp.where(r > 0.25, 0.5 - r, jnp.where(r < -0.25, -0.5 - r, r))
    v = r * (2.0 * math.pi)
    s = v * v
    p = -2.5052108e-8
    p = p * s + 2.7557319e-6
    p = p * s - 1.9841270e-4
    p = p * s + 8.3333333e-3
    p = p * s - 1.6666667e-1
    return v + v * s * p


def dot(a, b):
    return jnp.dot(a, b, preferred_element_type=F32)


def dot_nt(a, b):
    return lax.dot_general(a, b, (((1,), (1,)), ((), ())), preferred_element_type=F32)


def split2(v):
    hi = v.astype(BF)
    lo = (v - hi.astype(F32)).astype(BF)
    return hi, lo


def step_one_kernel(head_ref, q_ref, fwd_ref, inv_ref, field_ref, waves_ref, fx_ref, fxp_ref, fxi_ref, out_ref):
    head = head_ref[...]
    hx, hy, hz = head[:, 0:1], head[:, 1:2], head[:, 2:3]
    w = waves_ref[...]
    rest_re = hy * w[0:1] + hz * w[1:2]
    rest_im = hy * w[2:3] + hz * w[3:4]
    nyq_re = hy * w[4:5] + hz * w[5:6]
    nyq_im = hy * w[6:7] + hz * w[7:8]
    x_nyq = turns_sin(hx * -0.5)
    c_re, s_re, c_im = turns_cos(rest_re), turns_sin(rest_re), turns_cos(rest_im)
    cn_re, cn_im = turns_cos(nyq_re), turns_cos(nyq_im)
    sn_re, sn_im = turns_sin(nyq_re) * x_nyq, turns_sin(nyq_im) * x_nyq
    lane_m = lax.broadcasted_iota(jnp.int32, (8, 512), 1) // 64
    pick = (lax.broadcasted_iota(jnp.int32, (8, 512), 0) == lane_m).astype(BF)
    pick2 = jnp.concatenate([pick, pick], 0)

    def spread(tab):
        hi, lo = split2(tab.T)
        return dot(jnp.concatenate([hi, lo], 1), pick2)

    a = spread(c_re * cn_re).reshape(64, 8, 512)
    d = spread(c_im * cn_im).reshape(64, 8, 512)
    b = spread(s_re * cn_re).reshape(64, 8, 512)
    lane_j = lax.broadcasted_iota(jnp.int32, (8, 64), 1)
    freq = (lane_j % 32).astype(F32) * (1.0 / 64.0)
    is_nyq = lane_j == 32
    cx = jnp.where(is_nyq, turns_cos(hx * -0.5), turns_cos(hx * freq))
    sx = jnp.where(is_nyq, 0.0, turns_sin(hx * freq))
    rows = (fx_ref[...][None] * cx[:, None, :] + fxp_ref[...][None] * sx[:, None, :]).reshape(512, 64)
    hi, lo = split2(rows)
    inv8 = jnp.concatenate([fxi_ref[...]] * 8, 1)
    full = dot(hi, inv8) + dot(lo, inv8)
    row_m = lax.broadcasted_iota(jnp.int32, (512, 512), 0) // 64
    col_m = lax.broadcasted_iota(jnp.int32, (512, 512), 1) // 64
    same = row_m == col_m
    shift_x = jnp.where(same, full, 0.0).astype(BF)
    odd = (lax.broadcasted_iota(jnp.int32, (512, 512), 0) + lax.broadcasted_iota(jnp.int32, (512, 512), 1)) % 2
    nyq_x = jnp.where(same, jnp.where(odd == 1, 1.0 / 64, -1.0 / 64), 0.0).astype(BF)

    spec = dot_nt(fwd_ref[...], q_ref[...]).reshape(64, 2, 8, 512)
    re, im = spec[:, 0], spec[:, 1]
    u = jnp.stack([a * re + b * im, d * im - b * re], 1).reshape(1024, 512).astype(BF)
    ng = NYQUIST_ROWS // 16
    ta = spread(c_re * sn_re)[512 - 8 * ng :].reshape(ng, 8, 512)
    td = spread(c_im * sn_im)[512 - 8 * ng :].reshape(ng, 8, 512)
    tb = spread(s_re * sn_re)[512 - 8 * ng :].reshape(ng, 8, 512)
    ret, imt = re[64 - ng :], im[64 - ng :]
    tail = jnp.stack([ta * ret + tb * imt, td * imt - tb * ret], 1).reshape(NYQUIST_ROWS, 512).astype(BF)
    head_rows = dot(u[: 1024 - NYQUIST_ROWS], shift_x).astype(BF)
    tail_rows = (dot(u[1024 - NYQUIST_ROWS :], shift_x) + dot(tail, nyq_x)).astype(BF)
    turned = jnp.concatenate([head_rows, tail_rows], 0)
    damp = jnp.exp(-field_ref[...])
    damp = jnp.concatenate([damp, damp], 0).T
    damp = jnp.concatenate([damp] * 4, 1)
    moved = (dot(inv_ref[...], turned) * damp).astype(BF)
    out_ref[...] = dot(fwd_ref[...], moved).astype(BF).reshape(64, 16, 512)


def mix_kernel(head_ref, x_ref, d_ref, waves_ref, fx_ref, fxp_ref, fxi_ref, out_ref, wide_ref, mixed_ref):
    for quad in range(4):
        wide_ref[pl.ds(quad * 1024, 1024), :] = (
            x_ref[:, :, quad * 128 : (quad + 1) * 128].reshape(1024, 128).astype(F32)
        )
    left = lax.broadcasted_iota(jnp.int32, (64, 128), 1) < 64
    for pair in range(8):
        for quad in range(4):
            first = wide_ref[pl.ds(quad * 1024 + 2 * pair, 64, stride=16), :]
            second = wide_ref[pl.ds(quad * 1024 + 2 * pair + 1, 64, stride=16), :]
            even = jnp.where(left, first, pltpu.roll(second, 64, 1))
            odd = jnp.where(left, pltpu.roll(first, 64, 1), second)
            mixed_ref[pl.ds(2 * quad * 64, 64), pl.ds(pair * 128, 128)] = even.astype(BF)
            mixed_ref[pl.ds((2 * quad + 1) * 64, 64), pl.ds(pair * 128, 128)] = odd.astype(BF)
    dmat = d_ref[...]
    row = lax.broadcasted_iota(jnp.int32, (512, 512), 0)
    col = lax.broadcasted_iota(jnp.int32, (512, 512), 1)
    perm = ((row % 8) * 64 + row // 8 == col).astype(BF)
    d_first = dot(dmat, perm).astype(BF)
    mixed = dot(d_first, mixed_ref[...]).astype(BF)
    head = head_ref[...]
    hx, hy, hz = head[:, 0:1], head[:, 1:2], head[:, 2:3]
    lane = lax.broadcasted_iota(jnp.int32, (512, 128), 1) % 64
    freq = (lane % 32).astype(F32) * (1.0 / 64.0)
    is_nyq = lane == 32
    cx = jnp.where(is_nyq, 1.0, turns_cos(hx * freq))
    sx = jnp.where(is_nyq, 0.0, turns_sin(hx * freq))
    w = waves_ref[...]
    rest = hy * w[0:1] + hz * w[1:2]
    nyq = hx * w[4:5] + hy * w[2:3] + hz * w[3:4]
    cn = turns_cos(nyq)
    tc = turns_cos(rest) * cn
    ts = turns_sin(rest) * cn
    src = lax.broadcasted_iota(jnp.int32, (256, 512), 0) % 128
    dst = lax.broadcasted_iota(jnp.int32, (256, 512), 1)
    want = jnp.where(dst % 64 == 32, 16, 0) + dst // 64
    pick_re = (src == want).astype(BF)
    pick_im = (src == want + 8).astype(BF)
    tc2 = jnp.concatenate(split2(tc), 1)
    ts2 = jnp.concatenate(split2(ts), 1)
    a = dot(tc2, pick_re)
    d = dot(tc2, pick_im)
    b = dot(ts2, pick_re)
    cx = jnp.concatenate([cx] * 2, 1)
    sx = jnp.concatenate([sx] * 2, 1)
    parts = []
    for block in range(4):
        piece = mixed[:, block * 256 : (block + 1) * 256]
        parts.append(cx * dot(piece, fx_ref[...]) + sx * dot(piece, fxp_ref[...]))
    re = jnp.concatenate(parts[:2], 1)
    im = jnp.concatenate(parts[2:], 1)
    turned = jnp.concatenate([a * re + b * im, d * im - b * re], 1).astype(BF)
    last = dot(dmat, turned).astype(BF)
    out = dot_nt(fxi_ref[...], last).astype(BF).reshape(64, 16, 512)
    out_ref[0] = out[:, :, :256]
    out_ref[1] = out[:, :, 256:]


def moment_kernel(dir_ref, x_ref, inv_ref, field_ref, orient_ref, weight_ref, keep_ref, send_ref):
    first = dot(inv_ref[...], x_ref[0])
    second = dot(inv_ref[...], x_ref[1])
    hi, lo = split2(first * second)
    o = orient_ref[...]
    ux, uy, uz = o[0:1], o[1:2], o[2:3]
    rows = [jnp.ones_like(ux), ux * ux - THIRD, uy * uy - THIRD, ux * uy, ux * uz, uy * uz, 0.0 * ux, 0.0 * ux]
    g_hi, g_lo = split2(jnp.concatenate(rows, 0) * weight_ref[...])
    result = dot_nt(g_hi, hi) + dot_nt(g_hi, lo) + dot_nt(g_lo, hi)
    damp = jnp.exp(-field_ref[...])
    result = result * (damp * damp)
    is_first = dir_ref[0] == 0
    keep_ref[...] = jnp.where(is_first, result[:, :512], result[:, 512:])
    send_ref[...] = jnp.where(is_first, result[:, 512:], result[:, :512])


def group_waves(waves):
    table = np.zeros((64, 8, 128), np.float32)
    for group in range(64):
        cols = slice(group * 8, group * 8 + 8)
        for flag in range(2):
            for role in range(2):
                at = slice(flag * 16 + role * 8, flag * 16 + role * 8 + 8)
                table[group, 0, at] = waves[2 * role, cols]
                table[group, 1, at] = waves[2 * role + 1, cols]
                table[group, 2, at] = waves[4 + 2 * role, cols]
                table[group, 3, at] = waves[5 + 2 * role, cols]
                table[group, 4, at] = -0.5 * flag
    return table


def call(kernel, out_shape, args, scratch=(), smem_first=False):
    specs = [pl.BlockSpec(memory_space=pltpu.VMEM) for _ in args]
    if smem_first:
        specs[0] = pl.BlockSpec(memory_space=pltpu.SMEM)
    return pl.pallas_call(
        kernel,
        out_shape=out_shape,
        in_specs=specs,
        out_specs=jax.tree.map(lambda _: pl.BlockSpec(memory_space=pltpu.VMEM), out_shape),
        scratch_shapes=list(scratch),
        compiler_params=pltpu.CompilerParams(vmem_limit_bytes=VMEM_LIMIT),
    )(*args)


def on_device(propagators, field, orient, quad_weights, analysis, synthesis, decay):
    tab = tables()
    forward = jnp.asarray(tab["forward"].astype(BF))
    inverse = jnp.asarray(tab["inverse"].astype(BF))
    fx = jnp.asarray(tab["fx"].astype(np.float32))
    fxp = jnp.asarray(tab["fxp"].astype(np.float32))
    fxi = jnp.asarray(tab["fxi"].astype(BF))
    eye4 = np.eye(4)
    fx4 = jnp.asarray(np.kron(eye4, tab["fx"]).astype(BF))
    fxp4 = jnp.asarray(np.kron(eye4, tab["fxp"]).astype(BF))
    inv_x = np.zeros((64, 16, 16, 64))
    for r in range(16):
        inv_x[:, r, r, :] = tab["fxi"].T
    inv_x = jnp.asarray(inv_x.reshape(1024, 1024).astype(BF))
    shard = lax.axis_index("shard")
    direction = lax.axis_index("dir")
    heading = (orient * (TRANSPORT * (1.0 - 2.0 * direction.astype(F32)))).T
    local_heading = lax.dynamic_slice_in_dim(heading, shard * LOCAL, LOCAL, 0)
    state = propagators.reshape(LOCAL * NX, CELLS)
    first = call(
        step_one_kernel,
        jax.ShapeDtypeStruct((64, 16, 512), BF),
        (local_heading, state, forward, inverse, field, jnp.asarray(tab["waves"]), fx, fxp, fxi),
    )
    d_matrix = jnp.dot(
        synthesis, (analysis.astype(F32) * decay[:, None]).astype(BF), preferred_element_type=F32
    ).astype(BF)
    gathered = lax.all_to_all(first, "shard", split_axis=0, concat_axis=0, tiled=True)
    local_waves = lax.dynamic_index_in_dim(jnp.asarray(group_waves(tab["waves"])), shard, 0, False)
    mixed = call(
        mix_kernel,
        jax.ShapeDtypeStruct((2, 64, 16, 256), BF),
        (heading, gathered, d_matrix, local_waves, fx4, fxp4, inv_x),
        (pltpu.VMEM((4096, 128), F32), pltpu.VMEM((512, 1024), BF)),
    )
    planes = lax.all_to_all(
        mixed.reshape(128, 16, 256), ("dir", "shard"), split_axis=0, concat_axis=0, tiled=True
    ).reshape(2, 1024, 256)
    local_field = lax.dynamic_slice_in_dim(field, shard, 1, 0)
    half_orient = lax.dynamic_slice_in_dim(orient, direction * 256, 256, 1)
    half_weight = lax.dynamic_slice_in_dim(quad_weights, direction * 256, 256, 0)[None]
    keep, send = call(
        moment_kernel,
        (jax.ShapeDtypeStruct((8, 512), F32), jax.ShapeDtypeStruct((8, 512), F32)),
        (direction[None].astype(jnp.int32), planes, inverse, local_field, half_orient, half_weight),
        smem_first=True,
    )
    total = keep + lax.ppermute(send, "dir", [(0, 1), (1, 0)])
    return total[:1], total[1:6, None]


def solution(mesh):
    in_specs = (P("dir", "shard", None, None), P(), P(), P(), P(), P(), P())
    out_specs = (P("shard", "dir"), P(None, "shard", "dir"))
    return jax.shard_map(on_device, mesh=mesh, in_specs=in_specs, out_specs=out_specs, check_vma=False)
```

```python
import functools
import math

import jax
import jax.numpy as jnp
import numpy as np
from jax import lax
from jax.experimental import pallas as pl
from jax.experimental.pallas import tpu as pltpu
from jax.sharding import PartitionSpec as P

NX = 64
NY = 64
NZ = 16
M = 512
CELLS = NY * NZ
SHARDS = 64
LOCAL = M // SHARDS
TRANSPORT = 1.5
THIRD = 1.0 / 3.0
BF = jnp.bfloat16
F32 = jnp.float32


def slot_list():
    plain, nyquist = [], []
    for kz in range(1, 8):
        for ky in range(64):
            (nyquist if ky == 32 else plain).append(((ky, kz), (ky, kz), True))
    for ky in range(1, 32):
        plain.append(((ky, 0), (ky, 0), True))
        nyquist.append(((ky, 8), (ky, 8), True))
    nyquist.append(((0, 0), (0, 8), False))
    nyquist.append(((32, 0), (32, 8), False))
    return plain + nyquist


def point_waves(point):
    ky, kz = point
    fy = ky if ky <= 31 else ky - 64
    fz = kz if kz <= 7 else kz - 16
    rest = (0.0 if ky == 32 else fy / 64.0, 0.0 if kz == 8 else fz / 16.0)
    nyq = (-0.5 if ky == 32 else 0.0, -0.5 if kz == 8 else 0.0)
    return rest, nyq


@functools.lru_cache(maxsize=None)
def tables():
    slots = slot_list()
    y = np.arange(64)[:, None]
    z = np.arange(16)[None, :]
    forward = np.zeros((64, 2, 8, CELLS))
    weight = np.zeros((64, 2, 8))
    waves = np.zeros((8, 64, 2, 8), np.float32)
    for at, (re_point, im_point, paired) in enumerate(slots):
        group, slot = divmod(at, 8)
        for part, point in enumerate((re_point, im_point)):
            angle = 2.0 * math.pi * (((point[0] * y) % 64) / 64.0 + ((point[1] * z) % 16) / 16.0)
            row = -np.sin(angle) if (paired and part == 1) else np.cos(angle)
            forward[group, part, slot] = row.reshape(-1)
            weight[group, part, slot] = (2.0 if paired else 1.0) / CELLS
            rest, nyq = point_waves(point)
            waves[:5, group, part, slot] = rest + nyq + (weight[group, part, slot],)
    forward = forward.reshape(1024, CELLS)
    groups = np.zeros((64, 8, 128), np.float32)
    for group in range(64):
        for flag in range(2):
            groups[group, :4, flag * 16 : flag * 16 + 16] = waves[:4, group].reshape(4, 16)
            groups[group, 4, flag * 16 : flag * 16 + 16] = -0.5 * flag
            groups[group, 5, flag * 16 : flag * 16 + 16] = waves[4, group].reshape(16)
    x = np.arange(64)[:, None]
    j = np.arange(32)[None, :]
    angle = 2.0 * math.pi * ((x * j) % 64) / 64.0
    cosine = np.cos(angle)
    sine = -np.sin(angle)
    partner_c, partner_s = sine.copy(), -cosine
    sine[:, 0] = (-1.0) ** np.arange(64)
    partner_s[:, 0] = 0.0
    partner_c[:, 0] = 0.0
    fx = np.concatenate([cosine, sine], 1)
    fx_partner = np.concatenate([partner_c, partner_s], 1)
    wx = np.full(64, 2.0 / 64)
    wx[0] = wx[32] = 1.0 / 64
    fx_inv = (fx * wx[None, :]).T
    inv_x = np.zeros((64, 16, 16, 64))
    for r in range(16):
        inv_x[:, r, r, :] = fx_inv.T
    eye4 = np.eye(4)
    half = lambda v: v.astype(np.float32).astype(BF)
    return dict(
        forward=half(forward.reshape(64, 2, 8, CELLS).transpose(1, 0, 2, 3).reshape(1024, CELLS)),
        waves=waves.transpose(0, 2, 1, 3).reshape(8, 1024),
        groups=groups,
        fx=fx.astype(np.float32),
        fxp=fx_partner.astype(np.float32),
        fxi=half(np.tile(fx_inv.T, (4, 1))),
        inv_x=half(inv_x.reshape(1024, 1024)),
        fx4=half(np.kron(eye4, fx)),
        fxp4=half(np.kron(eye4, fx_partner)),
    )


def turns_cos(t):
    return turns_sin(t + 0.25)


def turns_sin(t):
    r = t - jnp.round(t)
    r = jnp.where(r > 0.25, 0.5 - r, jnp.where(r < -0.25, -0.5 - r, r))
    v = r * (2.0 * math.pi)
    s = v * v
    p = -2.5052108e-8
    p = p * s + 2.7557319e-6
    p = p * s - 1.9841270e-4
    p = p * s + 8.3333333e-3
    p = p * s - 1.6666667e-1
    return v + v * s * p


def dot(a, b):
    return jnp.dot(a, b, preferred_element_type=F32)


def dot_nt(a, b):
    return lax.dot_general(a, b, (((1,), (1,)), ((), ())), preferred_element_type=F32)


def split2(v):
    hi = v.astype(BF)
    lo = (v - hi.astype(F32)).astype(BF)
    return hi, lo


def direction_scale():
    return TRANSPORT * (1.0 - 2.0 * lax.axis_index("dir").astype(F32))


def step_one_kernel(
    orient_ref, waves_ref, fx_ref, fxp_ref, fxi_ref, q_hbm, fwd_hbm, field_hbm,
    out_hbm, q_ref, fwd_ref, field_ref, turned_ref, moved_ref, out_ref, sems,
):
    order = [pl.ds(at, 256) for at in (0, 512, 256, 768)]
    copies = [pltpu.make_async_copy(q_hbm, q_ref, sems.at[4])]
    copies += [pltpu.make_async_copy(fwd_hbm.at[at], fwd_ref.at[at], sems.at[i]) for i, at in enumerate(order)]
    copies += [pltpu.make_async_copy(field_hbm, field_ref, sems.at[5])]
    for copy in copies:
        copy.start()
    mine = lax.axis_index("shard") * LOCAL + lax.broadcasted_iota(jnp.int32, (8, 512), 0)
    chosen = (lax.broadcasted_iota(jnp.int32, (8, 512), 1) == mine).astype(F32) * direction_scale()
    hx, hy, hz = [jnp.sum(chosen * orient_ref[i : i + 1, :], 1, keepdims=True) for i in range(3)]
    w = waves_ref[...]
    rest = hy * w[0:1] + hz * w[1:2]
    nyq = hy * w[2:3] + hz * w[3:4]
    c, s = turns_cos(rest) * w[4:5], turns_sin(rest) * w[4:5]
    cn, sn = turns_cos(nyq), turns_sin(nyq) * turns_sin(hx * -0.5)
    plain = c * cn, (s * cn)[:, :512]
    tail = c * sn, (s * sn)[:, :512]
    lane_j = lax.broadcasted_iota(jnp.int32, (8, 64), 1)
    freq = (lane_j % 32).astype(F32) * (1.0 / 64.0)
    is_nyq = lane_j == 32
    cx = jnp.where(is_nyq, turns_cos(hx * -0.5), turns_cos(hx * freq))
    sx = jnp.where(is_nyq, 0.0, turns_sin(hx * freq))
    iota_r = lax.broadcasted_iota(jnp.int32, (256, 256), 0)
    iota_c = lax.broadcasted_iota(jnp.int32, (256, 256), 1)
    same = iota_r // 64 == iota_c // 64
    twice = jnp.concatenate([fxi_ref[...]] * 2, 1)
    shift_x = []
    for i in range(2):
        rows = [fx_ref[...] * cx[m : m + 1] + fxp_ref[...] * sx[m : m + 1] for m in range(4 * i, 4 * i + 4)]
        rows2 = jnp.concatenate(split2(jnp.concatenate(rows, 0)), 1)
        shift_x.append(jnp.where(same, dot_nt(twice, rows2), 0.0).astype(BF))
    nyq_x = jnp.where(same, jnp.where((iota_r + iota_c) % 2 == 1, 1.0 / 64, -1.0 / 64), 0.0).astype(BF)

    def rotate(re, im, table, at, width):
        out_re, out_im = [], []
        for m in range(LOCAL):
            rows = slice(m * 64, m * 64 + 64)
            a = table[0][m : m + 1, at : at + width]
            d = table[0][m : m + 1, 512 + at : 512 + at + width]
            b = table[1][m : m + 1, at : at + width]
            out_re.append((a * re[rows] + b * im[rows]).astype(BF))
            out_im.append((d * im[rows] - b * re[rows]).astype(BF))
        return jnp.concatenate(out_re, 0), jnp.concatenate(out_im, 0)

    copies[0].wait()
    for block in range(2):
        at = block * 256
        copies[1 + 2 * block].wait()
        copies[2 + 2 * block].wait()
        re = dot_nt(q_ref[...], fwd_ref[at : at + 256, :])
        im = dot_nt(q_ref[...], fwd_ref[512 + at : 768 + at, :])
        u = rotate(re, im, plain, at, 256)
        for part in range(2):
            for i in range(2):
                rows = slice(i * 256, i * 256 + 256)
                done = dot(shift_x[i], u[part][rows])
                lanes = part * 512 + at
                if block == 1:
                    if i == 0:
                        extra = rotate(re[:, 128:], im[:, 128:], tail, 384, 128)
                    turned_ref[rows, lanes : lanes + 128] = done[:, :128].astype(BF)
                    more = done[:, 128:] + dot(nyq_x, extra[part][rows])
                    turned_ref[rows, lanes + 128 : lanes + 256] = more.astype(BF)
                else:
                    turned_ref[rows, lanes : lanes + 256] = done.astype(BF)
    copies[5].wait()
    damp = jnp.exp(-field_ref[...])
    sends = []
    for i in range(2):
        rows = slice(i * 256, i * 256 + 256)
        moved = dot(turned_ref[rows, :], fwd_ref[...])
        for m in range(4):
            moved_ref[i * 256 + m * 64 : i * 256 + m * 64 + 64, :] = (moved[m * 64 : m * 64 + 64] * damp).astype(BF)
        out = dot_nt(fwd_ref[...], moved_ref[rows, :]).astype(BF)
        lanes = pl.ds(i * 256, 256)
        for part in range(2):
            out_ref[:, part * 8 : part * 8 + 8, lanes] = out[part * 512 : part * 512 + 512].reshape(64, 8, 256)
        sends.append(pltpu.make_async_copy(out_ref.at[:, :, lanes], out_hbm.at[:, :, lanes], sems.at[6 + i]))
        sends[i].start()
    for send in sends:
        send.wait()


def prepare_kernel(
    orient_ref, synthesis_ref, analysis_ref, decay_ref, groups_ref, fwd_ref,
    d_first_ref, d_ref, tc_ref, ts_ref, cx_ref, sx_ref, inv_ref,
):
    inv_ref[...] = fwd_ref[...].T
    scaled = (analysis_ref[...].astype(F32) * decay_ref[...]).astype(BF)
    d_ref[...] = dot(synthesis_ref[...], scaled).astype(BF)
    row = lax.broadcasted_iota(jnp.int32, (512, 512), 0)
    col = lax.broadcasted_iota(jnp.int32, (512, 512), 1)
    perm = ((row % 8) * 64 + row // 8 == col).astype(BF)
    d_first_ref[...] = dot(d_ref[...], perm).astype(BF)
    o = orient_ref[...] * direction_scale()
    head = jnp.concatenate([o, o, o[:2]], 0).T
    hx, hy, hz = head[:, 0:1], head[:, 1:2], head[:, 2:3]
    lane = lax.broadcasted_iota(jnp.int32, (512, 128), 1) % 64
    freq = (lane % 32).astype(F32) * (1.0 / 64.0)
    is_nyq = lane == 32
    cx_ref[...] = jnp.where(is_nyq, 1.0, turns_cos(hx * freq))
    sx_ref[...] = jnp.where(is_nyq, 0.0, turns_sin(hx * freq))
    w = groups_ref[lax.axis_index("shard")]
    rest = hy * w[0:1] + hz * w[1:2]
    cn = turns_cos(hx * w[4:5] + hy * w[2:3] + hz * w[3:4]) * w[5:6]
    tc_ref[...] = jnp.concatenate(split2(turns_cos(rest) * cn), 1)
    ts_ref[...] = jnp.concatenate(split2(turns_sin(rest) * cn), 1)


def mix_kernel(
    x_ref, d_first_ref, d_ref, tc_ref, ts_ref, cx_ref, sx_ref, fx_hbm, fxp_hbm, fxi_hbm, out_ref,
    wide_ref, mixed_ref, turned_ref, last_ref, fx_ref, fxp_ref, fxi_ref, sems,
):
    pairs = [(fx_hbm, fx_ref), (fxp_hbm, fxp_ref), (fxi_hbm, fxi_ref)]
    copies = [pltpu.make_async_copy(src, dst, sems.at[i]) for i, (src, dst) in enumerate(pairs)]
    for copy in copies:
        copy.start()
    left = lax.broadcasted_iota(jnp.int32, (64, 128), 1) < 64
    for quad in range(4):
        wide_ref[quad] = x_ref[:, :, quad * 128 : (quad + 1) * 128].reshape(1024, 128).astype(F32)
        for pair in range(8):
            first = wide_ref[quad, pl.ds(2 * pair, 64, stride=16), :]
            second = wide_ref[quad, pl.ds(2 * pair + 1, 64, stride=16), :]
            even = jnp.where(left, first, pltpu.roll(second, 64, 1))
            odd = jnp.where(left, pltpu.roll(first, 64, 1), second)
            mixed_ref[pl.ds(2 * quad * 64, 64), pl.ds(pair * 128, 128)] = even.astype(BF)
            mixed_ref[pl.ds((2 * quad + 1) * 64, 64), pl.ds(pair * 128, 128)] = odd.astype(BF)
    for copy in copies[:2]:
        copy.wait()
    src = lax.broadcasted_iota(jnp.int32, (256, 256), 0) % 128
    dst = lax.broadcasted_iota(jnp.int32, (256, 256), 1)
    cx = jnp.concatenate([cx_ref[...]] * 2, 1)
    sx = jnp.concatenate([sx_ref[...]] * 2, 1)

    def turn(at):
        piece = dot(d_first_ref[...], mixed_ref[:, at : at + 256]).astype(BF)
        return cx * dot(piece, fx_ref[...]) + sx * dot(piece, fxp_ref[...])

    for part in range(2):
        want = jnp.where(dst % 64 == 32, 16, 0) + dst // 64 + 4 * part
        pick_re = (src == want).astype(BF)
        pick_im = (src == want + 8).astype(BF)
        a = dot(tc_ref[...], pick_re)
        d = dot(tc_ref[...], pick_im)
        b = dot(ts_ref[...], pick_re)
        at = part * 256
        re, im = turn(at), turn(at + 512)
        turned_ref[:, at : at + 256] = (a * re + b * im).astype(BF)
        turned_ref[:, at + 512 : at + 768] = (d * im - b * re).astype(BF)
    for part in range(2):
        at = part * 256
        last_ref[at : at + 256, :] = dot(d_ref[at : at + 256, :], turned_ref[...]).astype(BF)
        if part == 0:
            copies[2].wait()
        out = dot_nt(fxi_ref[...], last_ref[at : at + 256, :]).astype(BF)
        out_ref[part] = out.reshape(64, 16, 256)


def moment_kernel(x_ref, orient_ref, weight_ref, inv_ref, field_hbm, keep_ref, send_ref, field_ref, sem):
    shard = lax.axis_index("shard")
    base = pl.multiple_of(shard // 8 * 8, 8)
    copy = pltpu.make_async_copy(field_hbm.at[pl.ds(base, 8)], field_ref, sem)
    copy.start()
    first_half = lax.axis_index("dir") == 0
    pick = lambda v: jnp.where(first_half, v[:, :256], v[:, 256:])
    o = pick(orient_ref[...])
    ux, uy, uz = o[0:1], o[1:2], o[2:3]
    rows = [jnp.ones_like(ux), ux * ux - THIRD, uy * uy - THIRD, ux * uy, ux * uz, uy * uz, 0.0 * ux, 0.0 * ux]
    g = jnp.concatenate(rows, 0) * pick(weight_ref[...])
    g = jnp.concatenate([g, jnp.zeros((120, 256), F32)], 0).T
    g_hi, g_lo = split2(g)
    parts = []
    x = x_ref[...].reshape(2, 64, 2, 8, 256)
    x = [jnp.concatenate([x[p, :, 0].reshape(512, 256), x[p, :, 1].reshape(512, 256)], 0) for p in range(2)]
    for block in range(4):
        inv = inv_ref[block * 256 : block * 256 + 256, :]
        hi, lo = split2(dot(inv, x[0]) * dot(inv, x[1]))
        parts.append((dot(hi, g_hi) + dot(lo, g_hi) + dot(hi, g_lo)).T[:8])
    result = jnp.concatenate(parts, 1)
    copy.wait()
    damp = jnp.exp(-field_ref[pl.ds(shard - base, 1), :])
    result = result * (damp * damp)
    keep_ref[...] = jnp.where(first_half, result[:, :512], result[:, 512:])
    send_ref[...] = jnp.where(first_half, result[:, 512:], result[:, :512])


def finish_kernel(keep_ref, got_ref, density_ref, tensor_ref):
    total = keep_ref[...] + got_ref[...]
    density_ref[...] = total[:1]
    for row in range(5):
        tensor_ref[row] = total[row + 1 : row + 2]


def on_chip(value):
    return pltpu.with_memory_space_constraint(value, pltpu.VMEM)


def call(kernel, out_shape, args, in_hbm=(), scratch=(), hbm_out=False):
    return pl.pallas_call(
        kernel,
        out_shape=out_shape,
        in_specs=[pl.BlockSpec(memory_space=pl.ANY if i in in_hbm else pltpu.VMEM) for i in range(len(args))],
        out_specs=jax.tree.map(lambda _: pl.BlockSpec(memory_space=pl.ANY if hbm_out else pltpu.VMEM), out_shape),
        scratch_shapes=list(scratch),
        compiler_params=pltpu.CompilerParams(vmem_limit_bytes=56 * 1024 * 1024),
    )(*args)


def on_device(propagators, field, orient, quad_weights, analysis, synthesis, decay):
    tab = {name: jnp.asarray(value) for name, value in tables().items()}
    sds, vm = jax.ShapeDtypeStruct, pltpu.VMEM
    state = propagators.reshape(LOCAL * NX, CELLS)
    first = call(
        step_one_kernel,
        sds((64, 16, 512), BF),
        (orient, tab["waves"], tab["fx"], tab["fxp"], tab["fxi"], state, tab["forward"], field),
        (5, 6, 7),
        (vm((512, 1024), BF), vm((1024, 1024), BF), vm((64, 1024), F32), vm((512, 1024), BF), vm((512, 1024), BF),
         vm((64, 16, 512), BF), pltpu.SemaphoreType.DMA((8,))),
        hbm_out=True,
    )
    gathered = lax.all_to_all(first, "shard", split_axis=0, concat_axis=0, tiled=True)
    *prepared, inverse = call(
        prepare_kernel,
        (vm((512, 512), BF), vm((512, 512), BF), vm((512, 256), BF), vm((512, 256), BF),
         vm((512, 128), F32), vm((512, 128), F32), sds((1024, 1024), BF)),
        (orient, synthesis, analysis, decay[:, None], tab["groups"], tab["forward"]),
    )
    mixed = call(
        mix_kernel,
        vm((2, 64, 16, 256), BF),
        tuple(on_chip(v) for v in (gathered, *prepared)) + (tab["fx4"], tab["fxp4"], tab["inv_x"]),
        (7, 8, 9),
        (vm((4, 1024, 128), F32), vm((512, 1024), BF), vm((512, 1024), BF), vm((512, 1024), BF), vm((256, 256), BF),
         vm((256, 256), BF), vm((1024, 1024), BF), pltpu.SemaphoreType.DMA((3,))),
    )
    planes = lax.all_to_all(
        mixed.reshape(128, 16, 256), ("dir", "shard"), split_axis=0, concat_axis=0, tiled=True
    ).reshape(2, 1024, 256)
    keep, send = call(
        moment_kernel,
        (vm((8, 512), F32), vm((8, 512), F32)),
        (on_chip(planes), orient, quad_weights[None], on_chip(inverse), field),
        (4,),
        (vm((8, 1024), F32), pltpu.SemaphoreType.DMA),
    )
    got = lax.ppermute(send, "dir", [(0, 1), (1, 0)])
    density, tensor = call(finish_kernel, (sds((1, 512), F32), sds((5, 1, 512), F32)), (on_chip(keep), on_chip(got)))
    return density, tensor


def solution(mesh):
    in_specs = (P("dir", "shard", None, None), P(), P(), P(), P(), P(), P())
    out_specs = (P("shard", "dir"), P(None, "shard", "dir"))
    return jax.shard_map(on_device, mesh=mesh, in_specs=in_specs, out_specs=out_specs, check_vma=False)
```

```python
import functools
import math

import jax
import jax.numpy as jnp
import numpy as np
from jax import lax
from jax.experimental import pallas as pl
from jax.experimental.pallas import tpu as pltpu
from jax.sharding import PartitionSpec as P

NX = 64
NY = 64
NZ = 16
M = 512
CELLS = NY * NZ
SHARDS = 64
LOCAL = M // SHARDS
TRANSPORT = 1.5
THIRD = 1.0 / 3.0
BF = jnp.bfloat16
F32 = jnp.float32


def slot_list():
    plain, nyquist = [], []
    for kz in range(1, 8):
        for ky in range(64):
            (nyquist if ky == 32 else plain).append(((ky, kz), (ky, kz), True))
    for ky in range(1, 32):
        plain.append(((ky, 0), (ky, 0), True))
        nyquist.append(((ky, 8), (ky, 8), True))
    nyquist.append(((0, 0), (0, 8), False))
    nyquist.append(((32, 0), (32, 8), False))
    return plain + nyquist


def point_waves(point):
    ky, kz = point
    fy = ky if ky <= 31 else ky - 64
    fz = kz if kz <= 7 else kz - 16
    rest = (0.0 if ky == 32 else fy / 64.0, 0.0 if kz == 8 else fz / 16.0)
    nyq = (-0.5 if ky == 32 else 0.0, -0.5 if kz == 8 else 0.0)
    return rest, nyq


@functools.lru_cache(maxsize=None)
def tables():
    slots = slot_list()
    y = np.arange(64)[:, None]
    z = np.arange(16)[None, :]
    forward = np.zeros((64, 2, 8, CELLS))
    weight = np.zeros((64, 2, 8))
    waves = np.zeros((8, 64, 2, 8), np.float32)
    for at, (re_point, im_point, paired) in enumerate(slots):
        group, slot = divmod(at, 8)
        for part, point in enumerate((re_point, im_point)):
            angle = 2.0 * math.pi * (((point[0] * y) % 64) / 64.0 + ((point[1] * z) % 16) / 16.0)
            row = -np.sin(angle) if (paired and part == 1) else np.cos(angle)
            forward[group, part, slot] = row.reshape(-1)
            weight[group, part, slot] = (2.0 if paired else 1.0) / CELLS
            rest, nyq = point_waves(point)
            waves[:5, group, part, slot] = rest + nyq + (weight[group, part, slot],)
    forward = forward.reshape(1024, CELLS)
    groups = np.zeros((64, 8, 128), np.float32)
    for group in range(64):
        for flag in range(2):
            groups[group, :4, flag * 16 : flag * 16 + 16] = waves[:4, group].reshape(4, 16)
            groups[group, 4, flag * 16 : flag * 16 + 16] = -0.5 * flag
            groups[group, 5, flag * 16 : flag * 16 + 16] = waves[4, group].reshape(16)
    x = np.arange(64)[:, None]
    j = np.arange(32)[None, :]
    angle = 2.0 * math.pi * ((x * j) % 64) / 64.0
    cosine = np.cos(angle)
    sine = -np.sin(angle)
    partner_c, partner_s = sine.copy(), -cosine
    sine[:, 0] = (-1.0) ** np.arange(64)
    partner_s[:, 0] = 0.0
    partner_c[:, 0] = 0.0
    fx = np.concatenate([cosine, sine], 1)
    fx_partner = np.concatenate([partner_c, partner_s], 1)
    wx = np.full(64, 2.0 / 64)
    wx[0] = wx[32] = 1.0 / 64
    fx_inv = (fx * wx[None, :]).T
    inv_x = np.zeros((64, 16, 16, 64))
    for r in range(16):
        inv_x[:, r, r, :] = fx_inv.T
    eye4 = np.eye(4)
    half = lambda v: v.astype(np.float32).astype(BF)
    return dict(
        forward=half(forward.reshape(64, 2, 8, CELLS).transpose(1, 0, 2, 3).reshape(1024, CELLS)),
        waves=waves.transpose(0, 2, 1, 3).reshape(8, 1024),
        groups=groups,
        fx=fx.astype(np.float32),
        fxp=fx_partner.astype(np.float32),
        fxi=half(np.tile(fx_inv.T, (4, 1))),
        inv_x=half(inv_x.reshape(1024, 1024)),
        fx8=half(np.concatenate([np.kron(eye4, fx), np.kron(eye4, fx_partner)], 1)),
    )


def turns_cos(t):
    return turns_sin(t + 0.25)


def turns_sin(t):
    r = t - jnp.round(t)
    r = jnp.where(r > 0.25, 0.5 - r, jnp.where(r < -0.25, -0.5 - r, r))
    v = r * (2.0 * math.pi)
    s = v * v
    p = -2.5052108e-8
    p = p * s + 2.7557319e-6
    p = p * s - 1.9841270e-4
    p = p * s + 8.3333333e-3
    p = p * s - 1.6666667e-1
    return v + v * s * p


def dot(a, b):
    return jnp.dot(a, b, preferred_element_type=F32)


def dot_nt(a, b):
    return lax.dot_general(a, b, (((1,), (1,)), ((), ())), preferred_element_type=F32)


def split2(v):
    hi = v.astype(BF)
    lo = (v - hi.astype(F32)).astype(BF)
    return hi, lo


def direction_scale():
    return TRANSPORT * (1.0 - 2.0 * lax.axis_index("dir").astype(F32))


def step_one_kernel(
    orient_ref, waves_ref, fx_ref, fxp_ref, fxi_ref, q_hbm, fwd_hbm, field_hbm,
    out_hbm, q_ref, fwd_ref, field_ref, turned_ref, moved_ref, out_ref, sems,
):
    order = [pl.ds(at, 256) for at in (0, 512, 256, 768)]
    copies = [pltpu.make_async_copy(q_hbm, q_ref, sems.at[4])]
    copies += [pltpu.make_async_copy(fwd_hbm.at[at], fwd_ref.at[at], sems.at[i]) for i, at in enumerate(order)]
    copies += [pltpu.make_async_copy(field_hbm, field_ref, sems.at[5])]
    for copy in copies[:3]:
        copy.start()
    mine = lax.axis_index("shard") * LOCAL + lax.broadcasted_iota(jnp.int32, (8, 512), 0)
    chosen = (lax.broadcasted_iota(jnp.int32, (8, 512), 1) == mine).astype(F32) * direction_scale()
    hx, hy, hz = [jnp.sum(chosen * orient_ref[i : i + 1, :], 1, keepdims=True) for i in range(3)]
    w = waves_ref[...]
    rest = hy * w[0:1] + hz * w[1:2]
    nyq = hy * w[2:3] + hz * w[3:4]
    c, s = turns_cos(rest) * w[4:5], turns_sin(rest) * w[4:5]
    cn, sn = turns_cos(nyq), turns_sin(nyq) * turns_sin(hx * -0.5)
    plain = c * cn, (s * cn)[:, :512]
    tail = c * sn, (s * sn)[:, :512]
    lane_j = lax.broadcasted_iota(jnp.int32, (8, 64), 1)
    freq = (lane_j % 32).astype(F32) * (1.0 / 64.0)
    is_nyq = lane_j == 32
    cx = jnp.where(is_nyq, turns_cos(hx * -0.5), turns_cos(hx * freq))
    sx = jnp.where(is_nyq, 0.0, turns_sin(hx * freq))
    iota_r = lax.broadcasted_iota(jnp.int32, (256, 256), 0)
    iota_c = lax.broadcasted_iota(jnp.int32, (256, 256), 1)
    same = iota_r // 64 == iota_c // 64
    twice = jnp.concatenate([fxi_ref[...]] * 2, 1)
    shift_x = []
    for i in range(2):
        rows = [fx_ref[...] * cx[m : m + 1] + fxp_ref[...] * sx[m : m + 1] for m in range(4 * i, 4 * i + 4)]
        rows2 = jnp.concatenate(split2(jnp.concatenate(rows, 0)), 1)
        shift_x.append(jnp.where(same, dot_nt(twice, rows2), 0.0).astype(BF))
    nyq_x = jnp.where(same, jnp.where((iota_r + iota_c) % 2 == 1, 1.0 / 64, -1.0 / 64), 0.0).astype(BF)

    def rotate(re, im, table, at, width):
        out_re, out_im = [], []
        for m in range(LOCAL):
            rows = slice(m * 64, m * 64 + 64)
            a = table[0][m : m + 1, at : at + width]
            d = table[0][m : m + 1, 512 + at : 512 + at + width]
            b = table[1][m : m + 1, at : at + width]
            out_re.append((a * re[rows] + b * im[rows]).astype(BF))
            out_im.append((d * im[rows] - b * re[rows]).astype(BF))
        return jnp.concatenate(out_re, 0), jnp.concatenate(out_im, 0)

    copies[0].wait()
    for block in range(2):
        at = block * 256
        copies[1 + 2 * block].wait()
        copies[2 + 2 * block].wait()
        if block == 0:
            for copy in copies[3:]:
                copy.start()
        re = dot_nt(q_ref[...], fwd_ref[at : at + 256, :])
        im = dot_nt(q_ref[...], fwd_ref[512 + at : 768 + at, :])
        u = rotate(re, im, plain, at, 256)
        for part in range(2):
            for i in range(2):
                rows = slice(i * 256, i * 256 + 256)
                done = dot(shift_x[i], u[part][rows])
                lanes = part * 512 + at
                if block == 1:
                    if i == 0:
                        extra = rotate(re[:, 128:], im[:, 128:], tail, 384, 128)
                    turned_ref[rows, lanes : lanes + 128] = done[:, :128].astype(BF)
                    more = done[:, 128:] + dot(nyq_x, extra[part][rows])
                    turned_ref[rows, lanes + 128 : lanes + 256] = more.astype(BF)
                else:
                    turned_ref[rows, lanes : lanes + 256] = done.astype(BF)
    copies[5].wait()
    damp = jnp.exp(-field_ref[...])
    sends = []
    for i in range(2):
        rows = slice(i * 256, i * 256 + 256)
        moved = dot(turned_ref[rows, :], fwd_ref[...])
        for m in range(4):
            moved_ref[i * 256 + m * 64 : i * 256 + m * 64 + 64, :] = (moved[m * 64 : m * 64 + 64] * damp).astype(BF)
        lanes = pl.ds(i * 256, 256)
        for part in range(2):
            out = dot_nt(fwd_ref[part * 512 : part * 512 + 512, :], moved_ref[rows, :]).astype(BF)
            at = (slice(None), pl.ds(part * 8, 8), lanes)
            out_ref[at] = out.reshape(64, 8, 256)
            send = pltpu.make_async_copy(out_ref.at[at], out_hbm.at[at], sems.at[6 + 2 * i + part])
            send.start()
            sends.append(send)
    for send in sends:
        send.wait()


def prepare_kernel(
    orient_ref, synthesis_ref, analysis_ref, decay_ref, groups_ref, fwd_ref, weight_ref, field_ref,
    d_first_ref, d_ref, tc_ref, ts_ref, cx_ref, sx_ref, inv_ref, g_ref, damp_ref,
):
    first_half = lax.axis_index("dir") == 0
    pick = lambda v: jnp.where(first_half, v[:, :256], v[:, 256:])
    u = pick(orient_ref[...])
    ux, uy, uz = u[0:1], u[1:2], u[2:3]
    rows = [jnp.ones_like(ux), ux * ux - THIRD, uy * uy - THIRD, ux * uy, ux * uz, uy * uz, 0.0 * ux, 0.0 * ux]
    g = jnp.concatenate(rows, 0) * pick(weight_ref[...])
    g = jnp.concatenate([g, jnp.zeros((120, 256), F32)], 0).T
    g_hi, g_lo = split2(g)
    g_ref[...] = jnp.concatenate([g_hi, g_hi, g_lo], 0)
    damp = jnp.exp(-field_ref[pl.ds(lax.axis_index("shard"), 1), :])
    damp_ref[...] = damp * damp
    inv_ref[...] = fwd_ref[...].T
    scaled = (analysis_ref[...].astype(F32) * decay_ref[...]).astype(BF)
    d_ref[...] = dot(synthesis_ref[...], scaled).astype(BF)
    row = lax.broadcasted_iota(jnp.int32, (512, 512), 0)
    col = lax.broadcasted_iota(jnp.int32, (512, 512), 1)
    perm = ((row % 8) * 64 + row // 8 == col).astype(BF)
    d_first_ref[...] = dot(d_ref[...], perm).astype(BF)
    o = orient_ref[...] * direction_scale()
    head = jnp.concatenate([o, o, o[:2]], 0).T
    hx, hy, hz = head[:, 0:1], head[:, 1:2], head[:, 2:3]
    lane = lax.broadcasted_iota(jnp.int32, (512, 128), 1) % 64
    freq = (lane % 32).astype(F32) * (1.0 / 64.0)
    is_nyq = lane == 32
    cx_ref[...] = jnp.where(is_nyq, 1.0, turns_cos(hx * freq))
    sx_ref[...] = jnp.where(is_nyq, 0.0, turns_sin(hx * freq))
    w = groups_ref[lax.axis_index("shard")]
    rest = hy * w[0:1] + hz * w[1:2]
    cn = turns_cos(hx * w[4:5] + hy * w[2:3] + hz * w[3:4]) * w[5:6]
    tc_ref[...] = jnp.concatenate(split2(turns_cos(rest) * cn), 1)
    ts_ref[...] = jnp.concatenate(split2(turns_sin(rest) * cn), 1)


def mix_kernel(
    x_ref, d_first_ref, d_ref, tc_ref, ts_ref, cx_ref, sx_ref, fx_hbm, fxi_hbm, out_ref,
    wide_ref, mixed_ref, turned_ref, last_ref, fx_ref, fxi_ref, sems,
):
    pairs = [(fx_hbm, fx_ref), (fxi_hbm, fxi_ref)]
    copies = [pltpu.make_async_copy(src, dst, sems.at[i]) for i, (src, dst) in enumerate(pairs)]
    for copy in copies:
        copy.start()
    left = lax.broadcasted_iota(jnp.int32, (64, 128), 1) < 64
    for quad in range(4):
        wide_ref[quad] = x_ref[:, :, quad * 128 : (quad + 1) * 128].reshape(1024, 128).astype(F32)

    def arrange(block):
        for pair in (2 * block, 2 * block + 1):
            for quad in range(4):
                first = wide_ref[quad, pl.ds(2 * pair, 64, stride=16), :]
                second = wide_ref[quad, pl.ds(2 * pair + 1, 64, stride=16), :]
                even = jnp.where(left, first, pltpu.roll(second, 64, 1))
                odd = jnp.where(left, pltpu.roll(first, 64, 1), second)
                mixed_ref[pl.ds(2 * quad * 64, 64), pl.ds(pair * 128, 128)] = even.astype(BF)
                mixed_ref[pl.ds((2 * quad + 1) * 64, 64), pl.ds(pair * 128, 128)] = odd.astype(BF)

    arrange(0)
    arrange(2)
    copies[0].wait()
    src = lax.broadcasted_iota(jnp.int32, (256, 256), 0) % 128
    dst = lax.broadcasted_iota(jnp.int32, (256, 256), 1)
    cx = jnp.concatenate([cx_ref[...]] * 2, 1)
    sx = jnp.concatenate([sx_ref[...]] * 2, 1)

    def turn(at):
        piece = dot(d_first_ref[...], mixed_ref[:, at : at + 256]).astype(BF)
        both = dot(piece, fx_ref[...])
        return cx * both[:, :256] + sx * both[:, 256:]

    for part in range(2):
        want = jnp.where(dst % 64 == 32, 16, 0) + dst // 64 + 4 * part
        pick_re = (src == want).astype(BF)
        pick_im = (src == want + 8).astype(BF)
        a = dot(tc_ref[...], pick_re)
        d = dot(tc_ref[...], pick_im)
        b = dot(ts_ref[...], pick_re)
        at = part * 256
        if part == 1:
            arrange(1)
            arrange(3)
        re, im = turn(at), turn(at + 512)
        turned_ref[:, at : at + 256] = (a * re + b * im).astype(BF)
        turned_ref[:, at + 512 : at + 768] = (d * im - b * re).astype(BF)
    for part in range(2):
        at = part * 256
        last_ref[at : at + 256, :] = dot(d_ref[at : at + 256, :], turned_ref[...]).astype(BF)
        if part == 0:
            copies[1].wait()
        out = dot_nt(fxi_ref[...], last_ref[at : at + 256, :]).astype(BF)
        out_ref[part] = out.reshape(64, 16, 256)


def moment_kernel(own, x_ref, g_ref, damp_ref, inv_ref, out_ref):
    me = lax.axis_index("dir")
    base = pl.multiple_of((me if own else 1 - me) * 512, 512)
    x = x_ref[...].reshape(2, 64, 2, 8, 256)
    x = [jnp.concatenate([x[p, :, 0].reshape(512, 256), x[p, :, 1].reshape(512, 256)], 0) for p in range(2)]
    parts = []
    for block in range(2):
        inv = inv_ref[pl.ds(base + block * 256, 256), :]
        hi, lo = split2(dot(inv, x[0]) * dot(inv, x[1]))
        parts.append(dot(jnp.concatenate([hi, lo, hi], 1), g_ref[...]).T[:8])
    out_ref[...] = jnp.concatenate(parts, 1) * damp_ref[:, pl.ds(base, 512)]


def finish_kernel(keep_ref, got_ref, density_ref, tensor_ref):
    total = keep_ref[...] + got_ref[...]
    density_ref[...] = total[:1]
    for row in range(5):
        tensor_ref[row] = total[row + 1 : row + 2]


def on_chip(value):
    return pltpu.with_memory_space_constraint(value, pltpu.VMEM)


def call(kernel, out_shape, args, in_hbm=(), scratch=(), hbm_out=False):
    return pl.pallas_call(
        kernel,
        out_shape=out_shape,
        in_specs=[pl.BlockSpec(memory_space=pl.ANY if i in in_hbm else pltpu.VMEM) for i in range(len(args))],
        out_specs=jax.tree.map(lambda _: pl.BlockSpec(memory_space=pl.ANY if hbm_out else pltpu.VMEM), out_shape),
        scratch_shapes=list(scratch),
        compiler_params=pltpu.CompilerParams(vmem_limit_bytes=56 * 1024 * 1024),
    )(*args)


def on_device(propagators, field, orient, quad_weights, analysis, synthesis, decay):
    tab = {name: jnp.asarray(value) for name, value in tables().items()}
    sds, vm = jax.ShapeDtypeStruct, pltpu.VMEM
    state = propagators.reshape(LOCAL * NX, CELLS)
    first = call(
        step_one_kernel,
        sds((64, 16, 512), BF),
        (orient, tab["waves"], tab["fx"], tab["fxp"], tab["fxi"], state, tab["forward"], field),
        (5, 6, 7),
        (vm((512, 1024), BF), vm((1024, 1024), BF), vm((64, 1024), F32), vm((512, 1024), BF), vm((512, 1024), BF),
         vm((64, 16, 512), BF), pltpu.SemaphoreType.DMA((10,))),
        hbm_out=True,
    )
    gathered = lax.all_to_all(first, "shard", split_axis=0, concat_axis=0, tiled=True)
    *prepared, inverse, g, damp = call(
        prepare_kernel,
        (vm((512, 512), BF), vm((512, 512), BF), vm((512, 256), BF), vm((512, 256), BF),
         vm((512, 128), F32), vm((512, 128), F32), sds((1024, 1024), BF),
         sds((768, 128), BF), sds((1, 1024), F32)),
        (orient, synthesis, analysis, decay[:, None], tab["groups"], tab["forward"], quad_weights[None], field),
    )
    mixed = call(
        mix_kernel,
        vm((2, 64, 16, 256), BF),
        tuple(on_chip(v) for v in (gathered, *prepared)) + (tab["fx8"], tab["inv_x"]),
        (7, 8),
        (vm((4, 1024, 128), F32), vm((512, 1024), BF), vm((512, 1024), BF), vm((512, 1024), BF), vm((256, 512), BF),
         vm((1024, 1024), BF), pltpu.SemaphoreType.DMA((2,))),
    )
    planes = lax.all_to_all(
        mixed.reshape(128, 16, 256), ("dir", "shard"), split_axis=0, concat_axis=0, tiled=True
    ).reshape(2, 1024, 256)
    operands = tuple(on_chip(v) for v in (planes, g, damp, inverse))
    send = call(functools.partial(moment_kernel, False), vm((8, 512), F32), operands)
    got = lax.ppermute(send, "dir", [(0, 1), (1, 0)])
    keep = call(functools.partial(moment_kernel, True), vm((8, 512), F32), operands)
    density, tensor = call(finish_kernel, (sds((1, 512), F32), sds((5, 1, 512), F32)), (on_chip(keep), on_chip(got)))
    return density, tensor


def solution(mesh):
    in_specs = (P("dir", "shard", None, None), P(), P(), P(), P(), P(), P())
    out_specs = (P("shard", "dir"), P(None, "shard", "dir"))
    return jax.shard_map(on_device, mesh=mesh, in_specs=in_specs, out_specs=out_specs, check_vma=False)
```

```python
import functools
import math

import jax
import jax.numpy as jnp
import numpy as np
from jax import lax
from jax.experimental import pallas as pl
from jax.experimental.pallas import tpu as pltpu
from jax.sharding import PartitionSpec as P

NX = 64
NY = 64
NZ = 16
M = 512
CELLS = NY * NZ
SHARDS = 64
LOCAL = M // SHARDS
TRANSPORT = 1.5
THIRD = 1.0 / 3.0
BF = jnp.bfloat16
F32 = jnp.float32


def slot_list():
    plain, nyquist = [], []
    for kz in range(1, 8):
        for ky in range(64):
            (nyquist if ky == 32 else plain).append(((ky, kz), (ky, kz), True))
    for ky in range(1, 32):
        plain.append(((ky, 0), (ky, 0), True))
        nyquist.append(((ky, 8), (ky, 8), True))
    nyquist.append(((0, 0), (0, 8), False))
    nyquist.append(((32, 0), (32, 8), False))
    return plain + nyquist


def point_waves(point):
    ky, kz = point
    fy = ky if ky <= 31 else ky - 64
    fz = kz if kz <= 7 else kz - 16
    rest = (0.0 if ky == 32 else fy / 64.0, 0.0 if kz == 8 else fz / 16.0)
    nyq = (-0.5 if ky == 32 else 0.0, -0.5 if kz == 8 else 0.0)
    return rest, nyq


@functools.lru_cache(maxsize=None)
def tables():
    slots = slot_list()
    y = np.arange(64)[:, None]
    z = np.arange(16)[None, :]
    forward = np.zeros((64, 2, 8, CELLS))
    weight = np.zeros((64, 2, 8))
    waves = np.zeros((8, 64, 2, 8), np.float32)
    for at, (re_point, im_point, paired) in enumerate(slots):
        group, slot = divmod(at, 8)
        for part, point in enumerate((re_point, im_point)):
            angle = 2.0 * math.pi * (((point[0] * y) % 64) / 64.0 + ((point[1] * z) % 16) / 16.0)
            row = -np.sin(angle) if (paired and part == 1) else np.cos(angle)
            forward[group, part, slot] = row.reshape(-1)
            weight[group, part, slot] = (2.0 if paired else 1.0) / CELLS
            rest, nyq = point_waves(point)
            waves[:5, group, part, slot] = rest + nyq + (weight[group, part, slot],)
    forward = forward.reshape(1024, CELLS)
    groups = np.zeros((64, 8, 128), np.float32)
    for group in range(64):
        for flag in range(2):
            groups[group, :4, flag * 16 : flag * 16 + 16] = waves[:4, group].reshape(4, 16)
            groups[group, 4, flag * 16 : flag * 16 + 16] = -0.5 * flag
            groups[group, 5, flag * 16 : flag * 16 + 16] = waves[4, group].reshape(16)
    x = np.arange(64)[:, None]
    j = np.arange(32)[None, :]
    angle = 2.0 * math.pi * ((x * j) % 64) / 64.0
    cosine = np.cos(angle)
    sine = -np.sin(angle)
    partner_c, partner_s = sine.copy(), -cosine
    sine[:, 0] = (-1.0) ** np.arange(64)
    partner_s[:, 0] = 0.0
    partner_c[:, 0] = 0.0
    fx = np.concatenate([cosine, sine], 1)
    fx_partner = np.concatenate([partner_c, partner_s], 1)
    wx = np.full(64, 2.0 / 64)
    wx[0] = wx[32] = 1.0 / 64
    fx_inv = (fx * wx[None, :]).T
    inv_x = np.zeros((64, 16, 16, 64))
    for r in range(16):
        inv_x[:, r, r, :] = fx_inv.T
    eye4 = np.eye(4)
    half = lambda v: v.astype(np.float32).astype(BF)
    return dict(
        forward=half(forward.reshape(64, 2, 8, CELLS).transpose(1, 0, 2, 3).reshape(1024, CELLS)),
        waves=waves.transpose(0, 2, 1, 3).reshape(8, 1024),
        groups=groups,
        fx=np.stack([fx, fx_partner]).astype(np.float32),
        fxi=half(np.tile(fx_inv.T, (4, 1))),
        inv_x=half(inv_x.reshape(1024, 1024)),
        fx8=half(np.concatenate([np.kron(eye4, fx), np.kron(eye4, fx_partner)], 1)),
    )


def turns_cos(t):
    return turns_sin(t + 0.25)


def turns_sin(t):
    r = t - jnp.round(t)
    r = jnp.where(r > 0.25, 0.5 - r, jnp.where(r < -0.25, -0.5 - r, r))
    v = r * (2.0 * math.pi)
    s = v * v
    p = -2.5052108e-8
    p = p * s + 2.7557319e-6
    p = p * s - 1.9841270e-4
    p = p * s + 8.3333333e-3
    p = p * s - 1.6666667e-1
    return v + v * s * p


def dot(a, b):
    return jnp.dot(a, b, preferred_element_type=F32)


def dot_nt(a, b):
    return lax.dot_general(a, b, (((1,), (1,)), ((), ())), preferred_element_type=F32)


def split2(v):
    hi = v.astype(BF)
    lo = (v - hi.astype(F32)).astype(BF)
    return hi, lo


def direction_scale():
    return TRANSPORT * (1.0 - 2.0 * lax.axis_index("dir").astype(F32))


def step_one_kernel(
    orient_hbm, waves_hbm, fx_hbm, fxi_hbm, q_hbm, fwd_hbm, field_hbm, out_hbm,
    orient_ref, waves_ref, fx_ref, fxi_ref, q_ref, fwd_ref, field_ref, turned_ref, moved_ref, out_ref, sems,
):
    order = [pl.ds(at, 256) for at in (0, 512, 256, 768)]
    copies = [pltpu.make_async_copy(q_hbm, q_ref, sems.at[4])]
    copies += [pltpu.make_async_copy(fwd_hbm.at[at], fwd_ref.at[at], sems.at[i]) for i, at in enumerate(order)]
    copies += [pltpu.make_async_copy(field_hbm, field_ref, sems.at[5])]
    small = [
        pltpu.make_async_copy(src, dst, sems.at[10 + i])
        for i, (src, dst) in enumerate(
            [(orient_hbm, orient_ref), (waves_hbm, waves_ref), (fx_hbm, fx_ref), (fxi_hbm, fxi_ref)]
        )
    ]
    for copy in small + copies:
        copy.start()
    for copy in small:
        copy.wait()
    mine = lax.axis_index("shard") * LOCAL + lax.broadcasted_iota(jnp.int32, (8, 512), 0)
    chosen = (lax.broadcasted_iota(jnp.int32, (8, 512), 1) == mine).astype(F32) * direction_scale()
    hx, hy, hz = [jnp.sum(chosen * orient_ref[i : i + 1, :], 1, keepdims=True) for i in range(3)]
    w = waves_ref[...]
    rest = hy * w[0:1] + hz * w[1:2]
    nyq = hy * w[2:3] + hz * w[3:4]
    c, s = turns_cos(rest) * w[4:5], turns_sin(rest) * w[4:5]
    cn, sn = turns_cos(nyq), turns_sin(nyq) * turns_sin(hx * -0.5)
    plain = c * cn, (s * cn)[:, :512]
    tail = c * sn, (s * sn)[:, :512]
    lane_j = lax.broadcasted_iota(jnp.int32, (8, 64), 1)
    freq = (lane_j % 32).astype(F32) * (1.0 / 64.0)
    is_nyq = lane_j == 32
    cx = jnp.where(is_nyq, turns_cos(hx * -0.5), turns_cos(hx * freq))
    sx = jnp.where(is_nyq, 0.0, turns_sin(hx * freq))
    iota_r = lax.broadcasted_iota(jnp.int32, (256, 256), 0)
    iota_c = lax.broadcasted_iota(jnp.int32, (256, 256), 1)
    same = iota_r // 64 == iota_c // 64
    twice = jnp.concatenate([fxi_ref[...]] * 2, 1)
    shift_x = []
    for i in range(2):
        rows = [fx_ref[0] * cx[m : m + 1] + fx_ref[1] * sx[m : m + 1] for m in range(4 * i, 4 * i + 4)]
        rows2 = jnp.concatenate(split2(jnp.concatenate(rows, 0)), 1)
        shift_x.append(jnp.where(same, dot_nt(twice, rows2), 0.0).astype(BF))
    nyq_x = jnp.where(same, jnp.where((iota_r + iota_c) % 2 == 1, 1.0 / 64, -1.0 / 64), 0.0).astype(BF)

    def rotate(re, im, table, at, width):
        out_re, out_im = [], []
        for m in range(LOCAL):
            rows = slice(m * 64, m * 64 + 64)
            a = table[0][m : m + 1, at : at + width]
            d = table[0][m : m + 1, 512 + at : 512 + at + width]
            b = table[1][m : m + 1, at : at + width]
            out_re.append((a * re[rows] + b * im[rows]).astype(BF))
            out_im.append((d * im[rows] - b * re[rows]).astype(BF))
        return jnp.concatenate(out_re, 0), jnp.concatenate(out_im, 0)

    copies[0].wait()
    spec = []
    for block in range(2):
        at = block * 256
        copies[1 + 2 * block].wait()
        copies[2 + 2 * block].wait()
        spec.append([dot_nt(q_ref[...], fwd_ref[row : row + 256, :]) for row in (at, at + 512)])
    for block in range(2):
        at = block * 256
        re, im = spec[block]
        u = rotate(re, im, plain, at, 256)
        extra = rotate(re[:, 128:], im[:, 128:], tail, 384, 128) if block == 1 else None
        for part in range(2):
            for i in range(2):
                rows = slice(i * 256, i * 256 + 256)
                done = dot(shift_x[i], u[part][rows])
                lanes = part * 512 + at
                if block == 1:
                    turned_ref[rows, lanes : lanes + 128] = done[:, :128].astype(BF)
                    more = done[:, 128:] + dot(nyq_x, extra[part][rows])
                    turned_ref[rows, lanes + 128 : lanes + 256] = more.astype(BF)
                else:
                    turned_ref[rows, lanes : lanes + 256] = done.astype(BF)
    copies[5].wait()
    damp = jnp.exp(-field_ref[...])
    sends = []
    for i in range(2):
        rows = slice(i * 256, i * 256 + 256)
        moved = dot(turned_ref[rows, :], fwd_ref[...])
        for m in range(4):
            moved_ref[i * 256 + m * 64 : i * 256 + m * 64 + 64, :] = (moved[m * 64 : m * 64 + 64] * damp).astype(BF)
        lanes = pl.ds(i * 256, 256)
        for part in range(2):
            out = dot_nt(fwd_ref[part * 512 : part * 512 + 512, :], moved_ref[rows, :]).astype(BF)
            at = (slice(None), pl.ds(part * 8, 8), lanes)
            out_ref[at] = out.reshape(64, 8, 256)
            send = pltpu.make_async_copy(out_ref.at[at], out_hbm.at[at], sems.at[6 + 2 * i + part])
            send.start()
            sends.append(send)
    for send in sends:
        send.wait()


def prepare_kernel(
    orient_ref, synthesis_ref, analysis_ref, decay_ref, groups_ref, fwd_ref, weight_ref, field_ref,
    d_first_ref, d_ref, tc_ref, ts_ref, cx_ref, sx_ref, inv_ref, g_ref, damp_ref,
):
    first_half = lax.axis_index("dir") == 0
    pick = lambda v: jnp.where(first_half, v[:, :256], v[:, 256:])
    u = pick(orient_ref[...])
    ux, uy, uz = u[0:1], u[1:2], u[2:3]
    rows = [jnp.ones_like(ux), ux * ux - THIRD, uy * uy - THIRD, ux * uy, ux * uz, uy * uz, 0.0 * ux, 0.0 * ux]
    g = jnp.concatenate(rows, 0) * pick(weight_ref[...])
    g = jnp.concatenate([g, jnp.zeros((120, 256), F32)], 0).T
    g_hi, g_lo = split2(g)
    g_ref[...] = jnp.concatenate([g_hi, g_hi, g_lo], 0)
    damp = jnp.exp(-field_ref[pl.ds(lax.axis_index("shard"), 1), :])
    damp_ref[...] = damp * damp
    inv_ref[...] = fwd_ref[...].T
    scaled = (analysis_ref[...].astype(F32) * decay_ref[...]).astype(BF)
    d_ref[...] = dot(synthesis_ref[...], scaled).astype(BF)
    row = lax.broadcasted_iota(jnp.int32, (512, 512), 0)
    col = lax.broadcasted_iota(jnp.int32, (512, 512), 1)
    perm = ((row % 8) * 64 + row // 8 == col).astype(BF)
    d_first_ref[...] = dot(d_ref[...], perm).astype(BF)
    o = orient_ref[...] * direction_scale()
    head = jnp.concatenate([o, o, o[:2]], 0).T
    hx, hy, hz = head[:, 0:1], head[:, 1:2], head[:, 2:3]
    lane = lax.broadcasted_iota(jnp.int32, (512, 128), 1) % 64
    freq = (lane % 32).astype(F32) * (1.0 / 64.0)
    is_nyq = lane == 32
    cx_ref[...] = jnp.where(is_nyq, 1.0, turns_cos(hx * freq))
    sx_ref[...] = jnp.where(is_nyq, 0.0, turns_sin(hx * freq))
    w = groups_ref[lax.axis_index("shard")]
    rest = hy * w[0:1] + hz * w[1:2]
    cn = turns_cos(hx * w[4:5] + hy * w[2:3] + hz * w[3:4]) * w[5:6]
    tc_ref[...] = jnp.concatenate(split2(turns_cos(rest) * cn), 1)
    ts_ref[...] = jnp.concatenate(split2(turns_sin(rest) * cn), 1)


def mix_kernel(
    x_ref, d_first_ref, d_ref, tc_ref, ts_ref, cx_ref, sx_ref, fx_hbm, fxi_hbm, out_ref,
    wide_ref, mixed_ref, turned_ref, last_ref, fx_ref, fxi_ref, sems,
):
    pairs = [(fx_hbm, fx_ref), (fxi_hbm, fxi_ref)]
    copies = [pltpu.make_async_copy(src, dst, sems.at[i]) for i, (src, dst) in enumerate(pairs)]
    for copy in copies:
        copy.start()
    left = lax.broadcasted_iota(jnp.int32, (64, 128), 1) < 64
    for quad in range(4):
        wide_ref[quad] = x_ref[:, :, quad * 128 : (quad + 1) * 128].reshape(1024, 128).astype(F32)

    def arrange(block):
        for pair in (2 * block, 2 * block + 1):
            for quad in range(4):
                first = wide_ref[quad, pl.ds(2 * pair, 64, stride=16), :]
                second = wide_ref[quad, pl.ds(2 * pair + 1, 64, stride=16), :]
                even = jnp.where(left, first, pltpu.roll(second, 64, 1))
                odd = jnp.where(left, pltpu.roll(first, 64, 1), second)
                mixed_ref[pl.ds(2 * quad * 64, 64), pl.ds(pair * 128, 128)] = even.astype(BF)
                mixed_ref[pl.ds((2 * quad + 1) * 64, 64), pl.ds(pair * 128, 128)] = odd.astype(BF)

    copies[0].wait()
    arrange(0)
    arrange(2)
    src = lax.broadcasted_iota(jnp.int32, (256, 256), 0) % 128
    dst = lax.broadcasted_iota(jnp.int32, (256, 256), 1)
    cx = jnp.concatenate([cx_ref[...]] * 2, 1)
    sx = jnp.concatenate([sx_ref[...]] * 2, 1)

    def turn(at):
        piece = dot(d_first_ref[...], mixed_ref[:, at : at + 256]).astype(BF)
        both = dot(piece, fx_ref[...])
        return cx * both[:, :256] + sx * both[:, 256:]

    for part in range(2):
        want = jnp.where(dst % 64 == 32, 16, 0) + dst // 64 + 4 * part
        pick_re = (src == want).astype(BF)
        pick_im = (src == want + 8).astype(BF)
        a = dot(tc_ref[...], pick_re)
        d = dot(tc_ref[...], pick_im)
        b = dot(ts_ref[...], pick_re)
        at = part * 256
        if part == 1:
            arrange(1)
            arrange(3)
        re, im = turn(at), turn(at + 512)
        turned_ref[:, at : at + 256] = (a * re + b * im).astype(BF)
        turned_ref[:, at + 512 : at + 768] = (d * im - b * re).astype(BF)
    copies[1].wait()
    last_ref[...] = dot(d_ref[...], turned_ref[...]).astype(BF)
    for part in range(2):
        at = part * 256
        out = dot_nt(fxi_ref[...], last_ref[at : at + 256, :]).astype(BF)
        out_ref[part] = out.reshape(64, 16, 256)


def moment_kernel(own, x_ref, g_ref, damp_ref, inv_ref, out_ref):
    me = lax.axis_index("dir")
    base = pl.multiple_of((me if own else 1 - me) * 512, 512)
    x = x_ref[...].reshape(2, 64, 2, 8, 256)
    x = [jnp.concatenate([x[p, :, 0].reshape(512, 256), x[p, :, 1].reshape(512, 256)], 0) for p in range(2)]
    parts = []
    for block in range(2):
        inv = inv_ref[pl.ds(base + block * 256, 256), :]
        hi, lo = split2(dot(inv, x[0]) * dot(inv, x[1]))
        parts.append(dot(jnp.concatenate([hi, lo, hi], 1), g_ref[...]).T[:8])
    out_ref[...] = jnp.concatenate(parts, 1) * damp_ref[:, pl.ds(base, 512)]


def finish_kernel(keep_ref, got_ref, density_ref, tensor_ref):
    total = keep_ref[...] + got_ref[...]
    density_ref[...] = total[:1]
    for row in range(5):
        tensor_ref[row] = total[row + 1 : row + 2]


def on_chip(value):
    return pltpu.with_memory_space_constraint(value, pltpu.VMEM)


def call(kernel, out_shape, args, in_hbm=(), scratch=(), hbm_out=False):
    return pl.pallas_call(
        kernel,
        out_shape=out_shape,
        in_specs=[pl.BlockSpec(memory_space=pl.ANY if i in in_hbm else pltpu.VMEM) for i in range(len(args))],
        out_specs=jax.tree.map(lambda _: pl.BlockSpec(memory_space=pl.ANY if hbm_out else pltpu.VMEM), out_shape),
        scratch_shapes=list(scratch),
        compiler_params=pltpu.CompilerParams(vmem_limit_bytes=56 * 1024 * 1024),
    )(*args)


def on_device(propagators, field, orient, quad_weights, analysis, synthesis, decay):
    tab = {name: jnp.asarray(value) for name, value in tables().items()}
    sds, vm = jax.ShapeDtypeStruct, pltpu.VMEM
    state = propagators.reshape(LOCAL * NX, CELLS)
    first = call(
        step_one_kernel,
        sds((64, 16, 512), BF),
        (orient, tab["waves"], tab["fx"], tab["fxi"], state, tab["forward"], field),
        range(7),
        (vm((3, 512), F32), vm((8, 1024), F32), vm((2, 64, 64), F32), vm((256, 64), BF), vm((512, 1024), BF), vm((1024, 1024), BF), vm((64, 1024), F32), vm((512, 1024), BF), vm((512, 1024), BF),
         vm((64, 16, 512), BF), pltpu.SemaphoreType.DMA((14,))),
        hbm_out=True,
    )
    gathered = lax.all_to_all(first, "shard", split_axis=0, concat_axis=0, tiled=True)
    *prepared, inverse, g, damp = call(
        prepare_kernel,
        (vm((512, 512), BF), vm((512, 512), BF), vm((512, 256), BF), vm((512, 256), BF),
         vm((512, 128), F32), vm((512, 128), F32), sds((1024, 1024), BF),
         sds((768, 128), BF), sds((1, 1024), F32)),
        (orient, synthesis, analysis, decay[:, None], tab["groups"], tab["forward"], quad_weights[None], field),
    )
    mixed = call(
        mix_kernel,
        vm((2, 64, 16, 256), BF),
        tuple(on_chip(v) for v in (gathered, *prepared)) + (tab["fx8"], tab["inv_x"]),
        (7, 8),
        (vm((4, 1024, 128), F32), vm((512, 1024), BF), vm((512, 1024), BF), vm((512, 1024), BF), vm((256, 512), BF),
         vm((1024, 1024), BF), pltpu.SemaphoreType.DMA((2,))),
    )
    planes = lax.all_to_all(
        mixed.reshape(128, 16, 256), ("dir", "shard"), split_axis=0, concat_axis=0, tiled=True
    ).reshape(2, 1024, 256)
    operands = tuple(on_chip(v) for v in (planes, g, damp, inverse))
    send = call(functools.partial(moment_kernel, False), vm((8, 512), F32), operands)
    got = lax.ppermute(send, "dir", [(0, 1), (1, 0)])
    keep = call(functools.partial(moment_kernel, True), vm((8, 512), F32), operands)
    density, tensor = call(finish_kernel, (sds((1, 512), F32), sds((5, 1, 512), F32)), (on_chip(keep), on_chip(got)))
    return density, tensor


def solution(mesh):
    in_specs = (P("dir", "shard", None, None), P(), P(), P(), P(), P(), P())
    out_specs = (P("shard", "dir"), P(None, "shard", "dir"))
    return jax.shard_map(on_device, mesh=mesh, in_specs=in_specs, out_specs=out_specs, check_vma=False)
```

```python
import functools
import math

import jax
import jax.numpy as jnp
import numpy as np
from jax import lax
from jax.experimental import pallas as pl
from jax.experimental.pallas import tpu as pltpu
from jax.sharding import PartitionSpec as P

NX = 64
NY = 64
NZ = 16
M = 512
CELLS = NY * NZ
SHARDS = 64
LOCAL = M // SHARDS
TRANSPORT = 1.5
THIRD = 1.0 / 3.0
BF = jnp.bfloat16
F32 = jnp.float32


def slot_list():
    plain, nyquist = [], []
    for kz in range(1, 8):
        for ky in range(64):
            (nyquist if ky == 32 else plain).append(((ky, kz), (ky, kz), True))
    for ky in range(1, 32):
        plain.append(((ky, 0), (ky, 0), True))
        nyquist.append(((ky, 8), (ky, 8), True))
    nyquist.append(((0, 0), (0, 8), False))
    nyquist.append(((32, 0), (32, 8), False))
    return plain + nyquist


def point_waves(point):
    ky, kz = point
    fy = ky if ky <= 31 else ky - 64
    fz = kz if kz <= 7 else kz - 16
    rest = (0.0 if ky == 32 else fy / 64.0, 0.0 if kz == 8 else fz / 16.0)
    nyq = (-0.5 if ky == 32 else 0.0, -0.5 if kz == 8 else 0.0)
    return rest, nyq


@functools.lru_cache(maxsize=None)
def tables():
    slots = slot_list()
    y = np.arange(64)[:, None]
    z = np.arange(16)[None, :]
    forward = np.zeros((64, 2, 8, CELLS))
    weight = np.zeros((64, 2, 8))
    waves = np.zeros((8, 64, 2, 8), np.float32)
    for at, (re_point, im_point, paired) in enumerate(slots):
        group, slot = divmod(at, 8)
        for part, point in enumerate((re_point, im_point)):
            angle = 2.0 * math.pi * (((point[0] * y) % 64) / 64.0 + ((point[1] * z) % 16) / 16.0)
            row = -np.sin(angle) if (paired and part == 1) else np.cos(angle)
            forward[group, part, slot] = row.reshape(-1)
            weight[group, part, slot] = (2.0 if paired else 1.0) / CELLS
            rest, nyq = point_waves(point)
            waves[:5, group, part, slot] = rest + nyq + (weight[group, part, slot],)
    forward = forward.reshape(1024, CELLS)
    groups = np.zeros((64, 8, 128), np.float32)
    for group in range(64):
        for flag in range(2):
            groups[group, :4, flag * 16 : flag * 16 + 16] = waves[:4, group].reshape(4, 16)
            groups[group, 4, flag * 16 : flag * 16 + 16] = -0.5 * flag
            groups[group, 5, flag * 16 : flag * 16 + 16] = waves[4, group].reshape(16)
    x = np.arange(64)[:, None]
    j = np.arange(32)[None, :]
    angle = 2.0 * math.pi * ((x * j) % 64) / 64.0
    cosine = np.cos(angle)
    sine = -np.sin(angle)
    partner_c, partner_s = sine.copy(), -cosine
    sine[:, 0] = (-1.0) ** np.arange(64)
    partner_s[:, 0] = 0.0
    partner_c[:, 0] = 0.0
    fx = np.concatenate([cosine, sine], 1)
    fx_partner = np.concatenate([partner_c, partner_s], 1)
    wx = np.full(64, 2.0 / 64)
    wx[0] = wx[32] = 1.0 / 64
    fx_inv = (fx * wx[None, :]).T
    inv_x = np.zeros((64, 16, 16, 64))
    for r in range(16):
        inv_x[:, r, r, :] = fx_inv.T
    eye4 = np.eye(4)
    half = lambda v: v.astype(np.float32).astype(BF)
    return dict(
        forward=half(forward.reshape(64, 2, 8, CELLS).transpose(1, 0, 2, 3).reshape(1024, CELLS)),
        waves=waves.transpose(0, 2, 1, 3).reshape(8, 1024),
        groups=groups,
        fx=np.stack([fx, fx_partner]).astype(np.float32),
        fxi=half(np.tile(fx_inv.T, (4, 1))),
        inv_x=half(inv_x.reshape(1024, 1024)),
        fx8=half(np.concatenate([np.kron(eye4, fx), np.kron(eye4, fx_partner)], 1)),
    )


def turns_cos(t):
    return turns_sin(t + 0.25)


def turns_sin(t):
    r = t - jnp.round(t)
    r = jnp.where(r > 0.25, 0.5 - r, jnp.where(r < -0.25, -0.5 - r, r))
    v = r * (2.0 * math.pi)
    s = v * v
    p = -2.5052108e-8
    p = p * s + 2.7557319e-6
    p = p * s - 1.9841270e-4
    p = p * s + 8.3333333e-3
    p = p * s - 1.6666667e-1
    return v + v * s * p


def dot(a, b):
    return jnp.dot(a, b, preferred_element_type=F32)


def dot_nt(a, b):
    return lax.dot_general(a, b, (((1,), (1,)), ((), ())), preferred_element_type=F32)


def split2(v):
    hi = v.astype(BF)
    lo = (v - hi.astype(F32)).astype(BF)
    return hi, lo


CHIPS = ("xh", "y", "z", "core")


def shard_index():
    at = lax.axis_index
    return ((at("xh") * 4 + at("y")) * 4 + at("z")) * 2 + at("core")


def direction_scale():
    return TRANSPORT * (1.0 - 2.0 * lax.axis_index("dir").astype(F32))


def step_one_kernel(
    orient_hbm, waves_hbm, fx_hbm, fxi_hbm, q_hbm, fwd_hbm, field_hbm, out_hbm,
    orient_ref, waves_ref, fx_ref, fxi_ref, q_ref, fwd_ref, field_ref, turned_ref, moved_ref, out_ref, sems,
):
    order = [pl.ds(at, 256) for at in (0, 512, 256, 768)]
    copies = [pltpu.make_async_copy(q_hbm, q_ref, sems.at[4])]
    copies += [pltpu.make_async_copy(fwd_hbm.at[at], fwd_ref.at[at], sems.at[i]) for i, at in enumerate(order)]
    copies += [pltpu.make_async_copy(field_hbm, field_ref, sems.at[5])]
    small = [
        pltpu.make_async_copy(src, dst, sems.at[10 + i])
        for i, (src, dst) in enumerate(
            [(orient_hbm, orient_ref), (waves_hbm, waves_ref), (fx_hbm, fx_ref), (fxi_hbm, fxi_ref)]
        )
    ]
    for copy in small + copies:
        copy.start()
    for copy in small:
        copy.wait()
    mine = shard_index() * LOCAL + lax.broadcasted_iota(jnp.int32, (8, 512), 0)
    chosen = (lax.broadcasted_iota(jnp.int32, (8, 512), 1) == mine).astype(F32) * direction_scale()
    hx, hy, hz = [jnp.sum(chosen * orient_ref[i : i + 1, :], 1, keepdims=True) for i in range(3)]
    w = waves_ref[...]
    rest = hy * w[0:1] + hz * w[1:2]
    nyq = hy * w[2:3] + hz * w[3:4]
    c, s = turns_cos(rest) * w[4:5], turns_sin(rest) * w[4:5]
    cn, sn = turns_cos(nyq), turns_sin(nyq) * turns_sin(hx * -0.5)
    plain = c * cn, (s * cn)[:, :512]
    tail = c * sn, (s * sn)[:, :512]
    lane_j = lax.broadcasted_iota(jnp.int32, (8, 64), 1)
    freq = (lane_j % 32).astype(F32) * (1.0 / 64.0)
    is_nyq = lane_j == 32
    cx = jnp.where(is_nyq, turns_cos(hx * -0.5), turns_cos(hx * freq))
    sx = jnp.where(is_nyq, 0.0, turns_sin(hx * freq))
    iota_r = lax.broadcasted_iota(jnp.int32, (256, 256), 0)
    iota_c = lax.broadcasted_iota(jnp.int32, (256, 256), 1)
    same = iota_r // 64 == iota_c // 64
    twice = jnp.concatenate([fxi_ref[...]] * 2, 1)
    shift_x = []
    for i in range(2):
        rows = [fx_ref[0] * cx[m : m + 1] + fx_ref[1] * sx[m : m + 1] for m in range(4 * i, 4 * i + 4)]
        rows2 = jnp.concatenate(split2(jnp.concatenate(rows, 0)), 1)
        shift_x.append(jnp.where(same, dot_nt(twice, rows2), 0.0).astype(BF))
    nyq_x = jnp.where(same, jnp.where((iota_r + iota_c) % 2 == 1, 1.0 / 64, -1.0 / 64), 0.0).astype(BF)

    def rotate(re, im, table, at, width):
        out_re, out_im = [], []
        for m in range(LOCAL):
            rows = slice(m * 64, m * 64 + 64)
            a = table[0][m : m + 1, at : at + width]
            d = table[0][m : m + 1, 512 + at : 512 + at + width]
            b = table[1][m : m + 1, at : at + width]
            out_re.append((a * re[rows] + b * im[rows]).astype(BF))
            out_im.append((d * im[rows] - b * re[rows]).astype(BF))
        return jnp.concatenate(out_re, 0), jnp.concatenate(out_im, 0)

    copies[0].wait()
    spec = []
    for block in range(2):
        at = block * 256
        copies[1 + 2 * block].wait()
        copies[2 + 2 * block].wait()
        spec.append([dot_nt(q_ref[...], fwd_ref[row : row + 256, :]) for row in (at, at + 512)])
    for block in range(2):
        at = block * 256
        re, im = spec[block]
        u = rotate(re, im, plain, at, 256)
        extra = rotate(re[:, 128:], im[:, 128:], tail, 384, 128) if block == 1 else None
        for part in range(2):
            for i in range(2):
                rows = slice(i * 256, i * 256 + 256)
                done = dot(shift_x[i], u[part][rows])
                lanes = part * 512 + at
                if block == 1:
                    turned_ref[rows, lanes : lanes + 128] = done[:, :128].astype(BF)
                    more = done[:, 128:] + dot(nyq_x, extra[part][rows])
                    turned_ref[rows, lanes + 128 : lanes + 256] = more.astype(BF)
                else:
                    turned_ref[rows, lanes : lanes + 256] = done.astype(BF)
    copies[5].wait()
    damp = jnp.exp(-field_ref[...])
    sends = []
    for i in range(2):
        rows = slice(i * 256, i * 256 + 256)
        moved = dot(turned_ref[rows, :], fwd_ref[...])
        for m in range(4):
            moved_ref[i * 256 + m * 64 : i * 256 + m * 64 + 64, :] = (moved[m * 64 : m * 64 + 64] * damp).astype(BF)
        lanes = pl.ds(i * 256, 256)
        for part in range(2):
            out = dot_nt(fwd_ref[part * 512 : part * 512 + 512, :], moved_ref[rows, :]).astype(BF)
            at = (slice(None), pl.ds(part * 8, 8), lanes)
            out_ref[at] = out.reshape(64, 8, 256)
            send = pltpu.make_async_copy(out_ref.at[at], out_hbm.at[at], sems.at[6 + 2 * i + part])
            send.start()
            sends.append(send)
    for send in sends:
        send.wait()


def prepare_kernel(
    orient_ref, synthesis_ref, analysis_ref, decay_ref, groups_ref, fwd_ref, weight_ref, field_ref,
    d_first_ref, d_ref, tc_ref, ts_ref, cx_ref, sx_ref, inv_ref, g_ref, damp_ref,
):
    first_half = lax.axis_index("dir") == 0
    pick = lambda v: jnp.where(first_half, v[:, :256], v[:, 256:])
    u = pick(orient_ref[...])
    ux, uy, uz = u[0:1], u[1:2], u[2:3]
    rows = [jnp.ones_like(ux), ux * ux - THIRD, uy * uy - THIRD, ux * uy, ux * uz, uy * uz, 0.0 * ux, 0.0 * ux]
    g = jnp.concatenate(rows, 0) * pick(weight_ref[...])
    g = jnp.concatenate([g, jnp.zeros((120, 256), F32)], 0).T
    g_hi, g_lo = split2(g)
    g_ref[...] = jnp.concatenate([g_hi, g_hi, g_lo], 0)
    damp = jnp.exp(-field_ref[pl.ds(shard_index(), 1), :])
    damp_ref[...] = damp * damp
    inv_ref[...] = fwd_ref[...].T
    scaled = (analysis_ref[...].astype(F32) * decay_ref[...]).astype(BF)
    d_ref[...] = dot(synthesis_ref[...], scaled).astype(BF)
    row = lax.broadcasted_iota(jnp.int32, (512, 512), 0)
    col = lax.broadcasted_iota(jnp.int32, (512, 512), 1)
    perm = ((row % 8) * 64 + row // 8 == col).astype(BF)
    d_first_ref[...] = dot(d_ref[...], perm).astype(BF)
    o = orient_ref[...] * direction_scale()
    head = jnp.concatenate([o, o, o[:2]], 0).T
    hx, hy, hz = head[:, 0:1], head[:, 1:2], head[:, 2:3]
    lane = lax.broadcasted_iota(jnp.int32, (512, 128), 1) % 64
    freq = (lane % 32).astype(F32) * (1.0 / 64.0)
    is_nyq = lane == 32
    cx_ref[...] = jnp.where(is_nyq, 1.0, turns_cos(hx * freq))
    sx_ref[...] = jnp.where(is_nyq, 0.0, turns_sin(hx * freq))
    w = groups_ref[shard_index()]
    rest = hy * w[0:1] + hz * w[1:2]
    cn = turns_cos(hx * w[4:5] + hy * w[2:3] + hz * w[3:4]) * w[5:6]
    tc_ref[...] = jnp.concatenate(split2(turns_cos(rest) * cn), 1)
    ts_ref[...] = jnp.concatenate(split2(turns_sin(rest) * cn), 1)


def mix_kernel(
    x_ref, d_first_ref, d_ref, tc_ref, ts_ref, cx_ref, sx_ref, fx_hbm, fxi_hbm, out_ref,
    wide_ref, mixed_ref, turned_ref, last_ref, fx_ref, fxi_ref, sems,
):
    pairs = [(fx_hbm, fx_ref), (fxi_hbm, fxi_ref)]
    copies = [pltpu.make_async_copy(src, dst, sems.at[i]) for i, (src, dst) in enumerate(pairs)]
    for copy in copies:
        copy.start()
    left = lax.broadcasted_iota(jnp.int32, (64, 128), 1) < 64
    for quad in range(4):
        wide_ref[quad] = x_ref[:, :, quad * 128 : (quad + 1) * 128].reshape(1024, 128).astype(F32)

    def arrange(block):
        for pair in (2 * block, 2 * block + 1):
            for quad in range(4):
                first = wide_ref[quad, pl.ds(2 * pair, 64, stride=16), :]
                second = wide_ref[quad, pl.ds(2 * pair + 1, 64, stride=16), :]
                even = jnp.where(left, first, pltpu.roll(second, 64, 1))
                odd = jnp.where(left, pltpu.roll(first, 64, 1), second)
                mixed_ref[pl.ds(2 * quad * 64, 64), pl.ds(pair * 128, 128)] = even.astype(BF)
                mixed_ref[pl.ds((2 * quad + 1) * 64, 64), pl.ds(pair * 128, 128)] = odd.astype(BF)

    copies[0].wait()
    arrange(0)
    arrange(2)
    src = lax.broadcasted_iota(jnp.int32, (256, 256), 0) % 128
    dst = lax.broadcasted_iota(jnp.int32, (256, 256), 1)
    cx = jnp.concatenate([cx_ref[...]] * 2, 1)
    sx = jnp.concatenate([sx_ref[...]] * 2, 1)

    def turn(at):
        piece = dot(d_first_ref[...], mixed_ref[:, at : at + 256]).astype(BF)
        both = dot(piece, fx_ref[...])
        return cx * both[:, :256] + sx * both[:, 256:]

    for part in range(2):
        want = jnp.where(dst % 64 == 32, 16, 0) + dst // 64 + 4 * part
        pick_re = (src == want).astype(BF)
        pick_im = (src == want + 8).astype(BF)
        a = dot(tc_ref[...], pick_re)
        d = dot(tc_ref[...], pick_im)
        b = dot(ts_ref[...], pick_re)
        at = part * 256
        if part == 1:
            arrange(1)
            arrange(3)
        re, im = turn(at), turn(at + 512)
        turned_ref[:, at : at + 256] = (a * re + b * im).astype(BF)
        turned_ref[:, at + 512 : at + 768] = (d * im - b * re).astype(BF)
    copies[1].wait()
    last_ref[...] = dot(d_ref[...], turned_ref[...]).astype(BF)
    for part in range(2):
        at = part * 256
        out = dot_nt(fxi_ref[...], last_ref[at : at + 256, :]).astype(BF)
        out = out.reshape(32, 2, 16, 256)
        for core in range(2):
            out_ref[core, part] = out[:, core]


def moment_kernel(own, x_ref, g_ref, damp_ref, inv_ref, out_ref):
    me = lax.axis_index("dir")
    base = pl.multiple_of((me if own else 1 - me) * 512, 512)
    x = x_ref[...].reshape(2, 2, 32, 2, 8, 256)
    rows = lambda p, part: jnp.stack([x[0, p, :, part], x[1, p, :, part]], 1).reshape(512, 256)
    x = [jnp.concatenate([rows(p, 0), rows(p, 1)], 0) for p in range(2)]
    parts = []
    for block in range(2):
        inv = inv_ref[pl.ds(base + block * 256, 256), :]
        hi, lo = split2(dot(inv, x[0]) * dot(inv, x[1]))
        parts.append(dot(jnp.concatenate([hi, lo, hi], 1), g_ref[...]).T[:8])
    out_ref[...] = jnp.concatenate(parts, 1) * damp_ref[:, pl.ds(base, 512)]


def finish_kernel(keep_ref, got_ref, density_ref, tensor_ref):
    total = keep_ref[...] + got_ref[...]
    density_ref[...] = total[:1]
    for row in range(5):
        tensor_ref[row] = total[row + 1 : row + 2]


def on_chip(value):
    return pltpu.with_memory_space_constraint(value, pltpu.VMEM)


def call(kernel, out_shape, args, in_hbm=(), scratch=(), hbm_out=False):
    return pl.pallas_call(
        kernel,
        out_shape=out_shape,
        in_specs=[pl.BlockSpec(memory_space=pl.ANY if i in in_hbm else pltpu.VMEM) for i in range(len(args))],
        out_specs=jax.tree.map(lambda _: pl.BlockSpec(memory_space=pl.ANY if hbm_out else pltpu.VMEM), out_shape),
        scratch_shapes=list(scratch),
        compiler_params=pltpu.CompilerParams(vmem_limit_bytes=56 * 1024 * 1024),
    )(*args)


def on_device(propagators, field, orient, quad_weights, analysis, synthesis, decay):
    tab = {name: jnp.asarray(value) for name, value in tables().items()}
    sds, vm = jax.ShapeDtypeStruct, pltpu.VMEM
    state = propagators.reshape(LOCAL * NX, CELLS)
    first = call(
        step_one_kernel,
        sds((64, 16, 512), BF),
        (orient, tab["waves"], tab["fx"], tab["fxi"], state, tab["forward"], field),
        range(7),
        (vm((3, 512), F32), vm((8, 1024), F32), vm((2, 64, 64), F32), vm((256, 64), BF), vm((512, 1024), BF), vm((1024, 1024), BF), vm((64, 1024), F32), vm((512, 1024), BF), vm((512, 1024), BF),
         vm((64, 16, 512), BF), pltpu.SemaphoreType.DMA((14,))),
        hbm_out=True,
    )
    gathered = lax.all_to_all(first, CHIPS, split_axis=0, concat_axis=0, tiled=True)
    *prepared, inverse, g, damp = call(
        prepare_kernel,
        (vm((512, 512), BF), vm((512, 512), BF), vm((512, 256), BF), vm((512, 256), BF),
         vm((512, 128), F32), vm((512, 128), F32), sds((1024, 1024), BF),
         sds((768, 128), BF), sds((1, 1024), F32)),
        (orient, synthesis, analysis, decay[:, None], tab["groups"], tab["forward"], quad_weights[None], field),
    )
    mixed = call(
        mix_kernel,
        vm((2, 2, 32, 16, 256), BF),
        tuple(on_chip(v) for v in (gathered, *prepared)) + (tab["fx8"], tab["inv_x"]),
        (7, 8),
        (vm((4, 1024, 128), F32), vm((512, 1024), BF), vm((512, 1024), BF), vm((512, 1024), BF), vm((256, 512), BF),
         vm((1024, 1024), BF), pltpu.SemaphoreType.DMA((2,))),
    )
    planes = lax.all_to_all(
        mixed.reshape(128, 16, 256), ("core", "dir", "xh", "y", "z"), split_axis=0, concat_axis=0, tiled=True
    )
    operands = tuple(on_chip(v) for v in (planes, g, damp, inverse))
    send = call(functools.partial(moment_kernel, False), vm((8, 512), F32), operands)
    got = lax.ppermute(send, "dir", [(0, 1), (1, 0)])
    keep = call(functools.partial(moment_kernel, True), vm((8, 512), F32), operands)
    density, tensor = call(finish_kernel, (sds((1, 512), F32), sds((5, 1, 512), F32)), (on_chip(keep), on_chip(got)))
    return density, tensor


def solution(mesh):
    fine = jax.sharding.Mesh(mesh.devices.reshape(2, 2, 4, 4, 2), ("dir",) + CHIPS)
    in_specs = (P("dir", CHIPS, None, None), P(), P(), P(), P(), P(), P())
    out_specs = (P(CHIPS, "dir"), P(None, CHIPS, "dir"))
    return jax.shard_map(on_device, mesh=fine, in_specs=in_specs, out_specs=out_specs, check_vma=False)
```

```python
import functools
import math

import jax
import jax.numpy as jnp
import numpy as np
from jax import lax
from jax.experimental import pallas as pl
from jax.experimental.pallas import tpu as pltpu
from jax.sharding import PartitionSpec as P

NX = 64
NY = 64
NZ = 16
M = 512
CELLS = NY * NZ
SHARDS = 64
LOCAL = M // SHARDS
TRANSPORT = 1.5
THIRD = 1.0 / 3.0
BF = jnp.bfloat16
F32 = jnp.float32


def slot_list():
    plain, nyquist = [], []
    for kz in range(1, 8):
        for ky in range(64):
            (nyquist if ky == 32 else plain).append(((ky, kz), (ky, kz), True))
    for ky in range(1, 32):
        plain.append(((ky, 0), (ky, 0), True))
        nyquist.append(((ky, 8), (ky, 8), True))
    nyquist.append(((0, 0), (0, 8), False))
    nyquist.append(((32, 0), (32, 8), False))
    return plain + nyquist


def point_waves(point):
    ky, kz = point
    fy = ky if ky <= 31 else ky - 64
    fz = kz if kz <= 7 else kz - 16
    rest = (0.0 if ky == 32 else fy / 64.0, 0.0 if kz == 8 else fz / 16.0)
    nyq = (-0.5 if ky == 32 else 0.0, -0.5 if kz == 8 else 0.0)
    return rest, nyq


@functools.lru_cache(maxsize=None)
def tables():
    slots = slot_list()
    y = np.arange(64)[:, None]
    z = np.arange(16)[None, :]
    forward = np.zeros((64, 2, 8, CELLS))
    weight = np.zeros((64, 2, 8))
    waves = np.zeros((8, 64, 2, 8), np.float32)
    for at, (re_point, im_point, paired) in enumerate(slots):
        group, slot = divmod(at, 8)
        for part, point in enumerate((re_point, im_point)):
            angle = 2.0 * math.pi * (((point[0] * y) % 64) / 64.0 + ((point[1] * z) % 16) / 16.0)
            row = -np.sin(angle) if (paired and part == 1) else np.cos(angle)
            forward[group, part, slot] = row.reshape(-1)
            weight[group, part, slot] = (2.0 if paired else 1.0) / CELLS
            rest, nyq = point_waves(point)
            waves[:5, group, part, slot] = rest + nyq + (weight[group, part, slot],)
    forward = forward.reshape(1024, CELLS)
    groups = np.zeros((64, 8, 128), np.float32)
    for group in range(64):
        for flag in range(2):
            groups[group, :4, flag * 16 : flag * 16 + 16] = waves[:4, group].reshape(4, 16)
            groups[group, 4, flag * 16 : flag * 16 + 16] = -0.5 * flag
            groups[group, 5, flag * 16 : flag * 16 + 16] = waves[4, group].reshape(16)
    x = np.arange(64)[:, None]
    j = np.arange(32)[None, :]
    angle = 2.0 * math.pi * ((x * j) % 64) / 64.0
    cosine = np.cos(angle)
    sine = -np.sin(angle)
    partner_c, partner_s = sine.copy(), -cosine
    sine[:, 0] = (-1.0) ** np.arange(64)
    partner_s[:, 0] = 0.0
    partner_c[:, 0] = 0.0
    fx = np.concatenate([cosine, sine], 1)
    fx_partner = np.concatenate([partner_c, partner_s], 1)
    wx = np.full(64, 2.0 / 64)
    wx[0] = wx[32] = 1.0 / 64
    fx_inv = (fx * wx[None, :]).T
    inv_x = np.zeros((64, 16, 16, 64))
    for r in range(16):
        inv_x[:, r, r, :] = fx_inv.T
    eye4 = np.eye(4)
    half = lambda v: v.astype(np.float32).astype(BF)
    return dict(
        forward=half(forward.reshape(64, 2, 8, CELLS).transpose(1, 0, 2, 3).reshape(1024, CELLS)),
        waves=waves.transpose(0, 2, 1, 3).reshape(8, 1024),
        groups=groups,
        fx=np.stack([fx, fx_partner]).astype(np.float32),
        fxi=half(np.tile(fx_inv.T, (4, 1))),
        inv_x=half(inv_x.reshape(1024, 1024)),
        fx8=half(np.concatenate([np.kron(eye4, fx), np.kron(eye4, fx_partner)], 1)),
    )


def turns_cos(t):
    return turns_sin(t + 0.25)


def turns_sin(t):
    r = t - jnp.round(t)
    r = jnp.where(r > 0.25, 0.5 - r, jnp.where(r < -0.25, -0.5 - r, r))
    v = r * (2.0 * math.pi)
    s = v * v
    p = -2.5052108e-8
    p = p * s + 2.7557319e-6
    p = p * s - 1.9841270e-4
    p = p * s + 8.3333333e-3
    p = p * s - 1.6666667e-1
    return v + v * s * p


def dot(a, b):
    return jnp.dot(a, b, preferred_element_type=F32)


def dot_nt(a, b):
    return lax.dot_general(a, b, (((1,), (1,)), ((), ())), preferred_element_type=F32)


def split2(v):
    hi = v.astype(BF)
    lo = (v - hi.astype(F32)).astype(BF)
    return hi, lo


CHIPS = ("xh", "y", "z", "core")


def shard_index():
    at = lax.axis_index
    return ((at("xh") * 4 + at("y")) * 4 + at("z")) * 2 + at("core")


def direction_scale():
    return TRANSPORT * (1.0 - 2.0 * lax.axis_index("dir").astype(F32))


def step_one_kernel(
    orient_hbm, waves_hbm, fx_hbm, fxi_hbm, q_hbm, fwd_hbm, field_hbm, out_hbm,
    orient_ref, waves_ref, fx_ref, fxi_ref, q_ref, fwd_ref, field_ref, turned_ref, moved_ref, out_ref, sems,
):
    order = [pl.ds(at, 256) for at in (0, 512, 256, 768)]
    copies = [pltpu.make_async_copy(q_hbm, q_ref, sems.at[4])]
    copies += [pltpu.make_async_copy(fwd_hbm.at[at], fwd_ref.at[at], sems.at[i]) for i, at in enumerate(order)]
    copies += [pltpu.make_async_copy(field_hbm, field_ref, sems.at[5])]
    small = [
        pltpu.make_async_copy(src, dst, sems.at[10 + i])
        for i, (src, dst) in enumerate(
            [(orient_hbm, orient_ref), (waves_hbm, waves_ref), (fx_hbm, fx_ref), (fxi_hbm, fxi_ref)]
        )
    ]
    for copy in small + copies:
        copy.start()
    for copy in small:
        copy.wait()
    mine = shard_index() * LOCAL + lax.broadcasted_iota(jnp.int32, (8, 512), 0)
    chosen = (lax.broadcasted_iota(jnp.int32, (8, 512), 1) == mine).astype(F32) * direction_scale()
    hx, hy, hz = [jnp.sum(chosen * orient_ref[i : i + 1, :], 1, keepdims=True) for i in range(3)]
    w = waves_ref[...]
    rest = hy * w[0:1] + hz * w[1:2]
    nyq = hy * w[2:3] + hz * w[3:4]
    c, s = turns_cos(rest) * w[4:5], turns_sin(rest) * w[4:5]
    cn, sn = turns_cos(nyq), turns_sin(nyq) * turns_sin(hx * -0.5)
    plain = c * cn, (s * cn)[:, :512]
    tail = c * sn, (s * sn)[:, :512]
    lane_j = lax.broadcasted_iota(jnp.int32, (8, 64), 1)
    freq = (lane_j % 32).astype(F32) * (1.0 / 64.0)
    is_nyq = lane_j == 32
    cx = jnp.where(is_nyq, turns_cos(hx * -0.5), turns_cos(hx * freq))
    sx = jnp.where(is_nyq, 0.0, turns_sin(hx * freq))
    iota_r = lax.broadcasted_iota(jnp.int32, (256, 256), 0)
    iota_c = lax.broadcasted_iota(jnp.int32, (256, 256), 1)
    same = iota_r // 64 == iota_c // 64
    twice = jnp.concatenate([fxi_ref[...]] * 2, 1)
    shift_x = []
    for i in range(2):
        rows = [fx_ref[0] * cx[m : m + 1] + fx_ref[1] * sx[m : m + 1] for m in range(4 * i, 4 * i + 4)]
        rows2 = jnp.concatenate(split2(jnp.concatenate(rows, 0)), 1)
        shift_x.append(jnp.where(same, dot_nt(twice, rows2), 0.0).astype(BF))
    nyq_x = jnp.where(same, jnp.where((iota_r + iota_c) % 2 == 1, 1.0 / 64, -1.0 / 64), 0.0).astype(BF)

    def rotate(re, im, table, at, width):
        out_re, out_im = [], []
        for m in range(LOCAL):
            rows = slice(m * 64, m * 64 + 64)
            a = table[0][m : m + 1, at : at + width]
            d = table[0][m : m + 1, 512 + at : 512 + at + width]
            b = table[1][m : m + 1, at : at + width]
            out_re.append((a * re[rows] + b * im[rows]).astype(BF))
            out_im.append((d * im[rows] - b * re[rows]).astype(BF))
        return jnp.concatenate(out_re, 0), jnp.concatenate(out_im, 0)

    copies[0].wait()
    spec = []
    for block in range(2):
        at = block * 256
        copies[1 + 2 * block].wait()
        copies[2 + 2 * block].wait()
        spec.append([dot_nt(q_ref[...], fwd_ref[row : row + 256, :]) for row in (at, at + 512)])
    for block in range(2):
        at = block * 256
        re, im = spec[block]
        u = rotate(re, im, plain, at, 256)
        extra = rotate(re[:, 128:], im[:, 128:], tail, 384, 128) if block == 1 else None
        for part in range(2):
            for i in range(2):
                rows = slice(i * 256, i * 256 + 256)
                done = dot(shift_x[i], u[part][rows])
                lanes = part * 512 + at
                if block == 1:
                    turned_ref[rows, lanes : lanes + 128] = done[:, :128].astype(BF)
                    more = done[:, 128:] + dot(nyq_x, extra[part][rows])
                    turned_ref[rows, lanes + 128 : lanes + 256] = more.astype(BF)
                else:
                    turned_ref[rows, lanes : lanes + 256] = done.astype(BF)
    copies[5].wait()
    damp = jnp.exp(-field_ref[...])
    sends = []
    for i in range(2):
        rows = slice(i * 256, i * 256 + 256)
        moved = dot(turned_ref[rows, :], fwd_ref[...])
        for m in range(4):
            moved_ref[i * 256 + m * 64 : i * 256 + m * 64 + 64, :] = (moved[m * 64 : m * 64 + 64] * damp).astype(BF)
        lanes = pl.ds(i * 256, 256)
        for part in range(2):
            out = dot_nt(fwd_ref[part * 512 : part * 512 + 512, :], moved_ref[rows, :]).astype(BF)
            at = (slice(None), pl.ds(part * 8, 8), lanes)
            out_ref[at] = out.reshape(64, 8, 256)
            send = pltpu.make_async_copy(out_ref.at[at], out_hbm.at[at], sems.at[6 + 2 * i + part])
            send.start()
            sends.append(send)
    for send in sends:
        send.wait()


def prepare_kernel(
    orient_ref, synthesis_ref, analysis_ref, decay_ref, groups_ref, fwd_ref, weight_ref, field_ref,
    d_first_ref, d_ref, tc_ref, ts_ref, cx_ref, sx_ref, inv_ref, g_ref, damp_ref,
):
    first_half = lax.axis_index("dir") == 0
    pick = lambda v: jnp.where(first_half, v[:, :256], v[:, 256:])
    u = pick(orient_ref[...])
    ux, uy, uz = u[0:1], u[1:2], u[2:3]
    rows = [jnp.ones_like(ux), ux * ux - THIRD, uy * uy - THIRD, ux * uy, ux * uz, uy * uz, 0.0 * ux, 0.0 * ux]
    g = jnp.concatenate(rows, 0) * pick(weight_ref[...])
    g = jnp.concatenate([g, jnp.zeros((120, 256), F32)], 0).T
    g_hi, g_lo = split2(g)
    g_ref[...] = jnp.concatenate([g_hi, g_hi, g_lo], 0)
    damp = jnp.exp(-field_ref[pl.ds(shard_index(), 1), :])
    damp_ref[...] = damp * damp
    inv_ref[...] = fwd_ref[...].T
    scaled = (analysis_ref[...].astype(F32) * decay_ref[...]).astype(BF)
    d_ref[...] = dot(synthesis_ref[...], scaled).astype(BF)
    row = lax.broadcasted_iota(jnp.int32, (512, 512), 0)
    col = lax.broadcasted_iota(jnp.int32, (512, 512), 1)
    perm = ((row % 8) * 64 + (row // 8) % 2 * 32 + row // 16 == col).astype(BF)
    d_first_ref[...] = dot(d_ref[...], perm).astype(BF)
    o = orient_ref[...] * direction_scale()
    head = jnp.concatenate([o, o, o[:2]], 0).T
    hx, hy, hz = head[:, 0:1], head[:, 1:2], head[:, 2:3]
    lane = lax.broadcasted_iota(jnp.int32, (512, 128), 1) % 64
    freq = (lane % 32).astype(F32) * (1.0 / 64.0)
    is_nyq = lane == 32
    cx_ref[...] = jnp.where(is_nyq, 1.0, turns_cos(hx * freq))
    sx_ref[...] = jnp.where(is_nyq, 0.0, turns_sin(hx * freq))
    w = groups_ref[lax.axis_index("core") * 32 + shard_index() // 2]
    rest = hy * w[0:1] + hz * w[1:2]
    cn = turns_cos(hx * w[4:5] + hy * w[2:3] + hz * w[3:4]) * w[5:6]
    tc_ref[...] = jnp.concatenate(split2(turns_cos(rest) * cn), 1)
    ts_ref[...] = jnp.concatenate(split2(turns_sin(rest) * cn), 1)


def mix_kernel(
    x_ref, d_first_ref, d_ref, tc_ref, ts_ref, cx_ref, sx_ref, fx_hbm, fxi_hbm, out_ref,
    wide_ref, mixed_ref, turned_ref, last_ref, fx_ref, fxi_ref, sems,
):
    pairs = [(fx_hbm, fx_ref), (fxi_hbm, fxi_ref)]
    copies = [pltpu.make_async_copy(src, dst, sems.at[i]) for i, (src, dst) in enumerate(pairs)]
    for copy in copies:
        copy.start()
    left = lax.broadcasted_iota(jnp.int32, (64, 128), 1) < 64
    for quad in range(4):
        wide_ref[quad] = x_ref[:, :, quad * 128 : (quad + 1) * 128].reshape(1024, 128).astype(F32)

    def arrange(block):
        for pair in (2 * block, 2 * block + 1):
            for quad in range(4):
                first = wide_ref[quad, pl.ds(2 * pair, 64, stride=16), :]
                second = wide_ref[quad, pl.ds(2 * pair + 1, 64, stride=16), :]
                even = jnp.where(left, first, pltpu.roll(second, 64, 1))
                odd = jnp.where(left, pltpu.roll(first, 64, 1), second)
                mixed_ref[pl.ds(2 * quad * 64, 64), pl.ds(pair * 128, 128)] = even.astype(BF)
                mixed_ref[pl.ds((2 * quad + 1) * 64, 64), pl.ds(pair * 128, 128)] = odd.astype(BF)

    copies[0].wait()
    arrange(0)
    arrange(2)
    src = lax.broadcasted_iota(jnp.int32, (256, 256), 0) % 128
    dst = lax.broadcasted_iota(jnp.int32, (256, 256), 1)
    cx = jnp.concatenate([cx_ref[...]] * 2, 1)
    sx = jnp.concatenate([sx_ref[...]] * 2, 1)

    def turn(at):
        piece = dot(d_first_ref[...], mixed_ref[:, at : at + 256]).astype(BF)
        both = dot(piece, fx_ref[...])
        return cx * both[:, :256] + sx * both[:, 256:]

    for part in range(2):
        want = jnp.where(dst % 64 == 32, 16, 0) + dst // 64 + 4 * part
        pick_re = (src == want).astype(BF)
        pick_im = (src == want + 8).astype(BF)
        a = dot(tc_ref[...], pick_re)
        d = dot(tc_ref[...], pick_im)
        b = dot(ts_ref[...], pick_re)
        at = part * 256
        if part == 1:
            arrange(1)
            arrange(3)
        re, im = turn(at), turn(at + 512)
        turned_ref[:, at : at + 256] = (a * re + b * im).astype(BF)
        turned_ref[:, at + 512 : at + 768] = (d * im - b * re).astype(BF)
    copies[1].wait()
    last_ref[...] = dot(d_ref[...], turned_ref[...]).astype(BF)
    for part in range(2):
        at = part * 256
        out = dot_nt(fxi_ref[...], last_ref[at : at + 256, :]).astype(BF)
        out = out.reshape(32, 2, 16, 256)
        for core in range(2):
            out_ref[core, part] = out[:, core]


def moment_kernel(own, x_ref, g_ref, damp_ref, inv_ref, out_ref):
    me = lax.axis_index("dir")
    base = pl.multiple_of((me if own else 1 - me) * 512, 512)
    x = x_ref[...].reshape(2, 2, 32, 2, 8, 256)
    rows = lambda p, part: jnp.concatenate([x[core, p, :, part].reshape(256, 256) for core in range(2)], 0)
    x = [jnp.concatenate([rows(p, 0), rows(p, 1)], 0) for p in range(2)]
    parts = []
    for block in range(2):
        inv = inv_ref[pl.ds(base + block * 256, 256), :]
        hi, lo = split2(dot(inv, x[0]) * dot(inv, x[1]))
        parts.append(dot(jnp.concatenate([hi, lo, hi], 1), g_ref[...]).T[:8])
    out_ref[...] = jnp.concatenate(parts, 1) * damp_ref[:, pl.ds(base, 512)]


def finish_kernel(keep_ref, got_ref, density_ref, tensor_ref):
    total = keep_ref[...] + got_ref[...]
    density_ref[...] = total[:1]
    for row in range(5):
        tensor_ref[row] = total[row + 1 : row + 2]


def on_chip(value):
    return pltpu.with_memory_space_constraint(value, pltpu.VMEM)


def call(kernel, out_shape, args, in_hbm=(), scratch=(), hbm_out=False):
    return pl.pallas_call(
        kernel,
        out_shape=out_shape,
        in_specs=[pl.BlockSpec(memory_space=pl.ANY if i in in_hbm else pltpu.VMEM) for i in range(len(args))],
        out_specs=jax.tree.map(lambda _: pl.BlockSpec(memory_space=pl.ANY if hbm_out else pltpu.VMEM), out_shape),
        scratch_shapes=list(scratch),
        compiler_params=pltpu.CompilerParams(vmem_limit_bytes=56 * 1024 * 1024),
    )(*args)


def on_device(propagators, field, orient, quad_weights, analysis, synthesis, decay):
    tab = {name: jnp.asarray(value) for name, value in tables().items()}
    sds, vm = jax.ShapeDtypeStruct, pltpu.VMEM
    state = propagators.reshape(LOCAL * NX, CELLS)
    first = call(
        step_one_kernel,
        sds((64, 16, 512), BF),
        (orient, tab["waves"], tab["fx"], tab["fxi"], state, tab["forward"], field),
        range(7),
        (vm((3, 512), F32), vm((8, 1024), F32), vm((2, 64, 64), F32), vm((256, 64), BF), vm((512, 1024), BF), vm((1024, 1024), BF), vm((64, 1024), F32), vm((512, 1024), BF), vm((512, 1024), BF),
         vm((64, 16, 512), BF), pltpu.SemaphoreType.DMA((14,))),
        hbm_out=True,
    )
    gathered = lax.all_to_all(first, ("core", "xh", "y", "z"), split_axis=0, concat_axis=0, tiled=True)
    *prepared, inverse, g, damp = call(
        prepare_kernel,
        (vm((512, 512), BF), vm((512, 512), BF), vm((512, 256), BF), vm((512, 256), BF),
         vm((512, 128), F32), vm((512, 128), F32), sds((1024, 1024), BF),
         sds((768, 128), BF), sds((1, 1024), F32)),
        (orient, synthesis, analysis, decay[:, None], tab["groups"], tab["forward"], quad_weights[None], field),
    )
    mixed = call(
        mix_kernel,
        vm((2, 2, 32, 16, 256), BF),
        tuple(on_chip(v) for v in (gathered, *prepared)) + (tab["fx8"], tab["inv_x"]),
        (7, 8),
        (vm((4, 1024, 128), F32), vm((512, 1024), BF), vm((512, 1024), BF), vm((512, 1024), BF), vm((256, 512), BF),
         vm((1024, 1024), BF), pltpu.SemaphoreType.DMA((2,))),
    )
    planes = lax.all_to_all(
        mixed.reshape(128, 16, 256), ("core", "dir", "xh", "y", "z"), split_axis=0, concat_axis=0, tiled=True
    )
    operands = tuple(on_chip(v) for v in (planes, g, damp, inverse))
    send = call(functools.partial(moment_kernel, False), vm((8, 512), F32), operands)
    got = lax.ppermute(send, "dir", [(0, 1), (1, 0)])
    keep = call(functools.partial(moment_kernel, True), vm((8, 512), F32), operands)
    density, tensor = call(finish_kernel, (sds((1, 512), F32), sds((5, 1, 512), F32)), (on_chip(keep), on_chip(got)))
    return density, tensor


def solution(mesh):
    fine = jax.sharding.Mesh(mesh.devices.reshape(2, 2, 4, 4, 2), ("dir",) + CHIPS)
    in_specs = (P("dir", CHIPS, None, None), P(), P(), P(), P(), P(), P())
    out_specs = (P(CHIPS, "dir"), P(None, CHIPS, "dir"))
    return jax.shard_map(on_device, mesh=fine, in_specs=in_specs, out_specs=out_specs, check_vma=False)
```
